32 devices in a mesh: group: 2 (over y), seq: 4 (over z), chan: 2 (over x), sub: 2 (over core).
Axes of the slice: x: 2, y: 2, z: 4, core: 2. Of those that a mesh axis runs over, the one named last changes fastest.
Arguments:
- atom_single: bfloat16 [12288, 128], P(('group', 'seq', 'chan', 'sub')), parts along dimension 0, may hold values from -6 to 6
- atom_token: int32 [12288], P(('group', 'seq', 'chan', 'sub')), parts along dimension 0, may hold values from 0 to 767, as said below
- token_atoms: int32 [1536], P(('group', 'seq', 'chan', 'sub')), parts along dimension 0, may hold values from 1 to 19, as said below
- window_offset: int32 [384], P(('group', 'seq', 'chan', 'sub')), parts along dimension 0, may hold values from 0 to 96
- token_pair: bfloat16 [1536, 64, 128], P(('group', 'seq', 'chan', 'sub')), parts along dimension 0, may hold values from -6 to 6
- w_zpair: bfloat16 [128, 16], replicated, may hold values from -0.5 to 0.5
- w_single: bfloat16 [2, 128, 16], replicated, may hold values from -0.5 to 0.5
- w_pair_mlp: bfloat16 [3, 16, 16], replicated, may hold values from -1.5 to 1.5
- w_bias: bfloat16 [3, 16, 4], replicated, may hold values from -1.5 to 1.5
- w_attn: bfloat16 [3, 4, 128, 128], replicated, may hold values from -0.5 to 0.5
- w_out: bfloat16 [3, 128, 128], replicated, may hold values from -0.5 to 0.5
- w_trans_in: bfloat16 [3, 2, 128, 256], replicated, may hold values from -0.5 to 0.5
- w_trans_out: bfloat16 [3, 256, 128], replicated, may hold values from -0.375 to 0.375
- w_token: bfloat16 [128, 768], replicated, may hold values from -0.5 to 0.5
Outputs:
- token_single: bfloat16 [1536, 768], P(('group', 'seq', 'chan', 'sub')), parts along dimension 0
- atom_out: bfloat16 [12288, 128], P(('group', 'seq', 'chan', 'sub')), parts along dimension 0
The draws below stay inside these ranges and needn't reach their ends.
There are 2 independent parts, one for each index of `group`. The reference program is written for one: setup_inputs(seed, part) draws one part's arguments, and reference() takes and returns one part's arrays. A program takes and returns all parts, laid end to end along the dimension named above; an argument that names none is the same for every part. Nothing has to cross between parts.
Inputs may be any that keep to these rules, and one draw needn't show every extreme that they name: atom_token is non-decreasing and gives each token t exactly token_atoms[t] consecutive atoms. `token_atoms`: the atoms of the first aligned block of 48 tokens begin at 0; those of every later block s begin 384 // 8 to 96 atoms after 384 s; all tokens together have 6144 atoms.
All inputs are finite; a program needn't handle non-finite values.
Results may differ from the reference program's by a relative error of at most 0.01.
Values may be sent and summed in bfloat16 or wider, within the bound.
No kernel may reach another device: no remote copies, remote signals or barrier semaphores. Data moves between devices by JAX's collectives and lax.ppermute only.
A program may use at most 64 MiB of HBM per device.

```python
import math
import jax
import jax.numpy as jnp
from jax import lax

C = 128
CP = 16
CZ = 128
HEADS = 4
TH = 256
CT = 768
BLOCKS = 3
QB = 32
KW = 128
ATOM_DEV = 384
HD = 32
HALO = 96
BANDW = 64
TOK_DEV = 48
SHARDS = 16
ATOMS = 6144
TOKENS = 768


def shared_counts(key):
    shards = TOKENS // TOK_DEV
    drift_key, order_key, place_key = jax.random.split(jax.random.fold_in(key, 11), 3)
    drift = jax.random.randint(drift_key, (shards + 1,), ATOM_DEV // 8, ATOM_DEV // 4 + 1).astype(jnp.int32)
    drift = drift.at[0].set(0)
    drift = drift.at[1].set(ATOM_DEV // 4)
    drift = drift.at[shards].set(0)
    totals = ATOM_DEV + drift[1:] - drift[:-1]
    single = TOK_DEV // 2
    others = TOK_DEV - single
    spare_atoms = totals - single
    floor_count = spare_atoms // others
    remain = spare_atoms % others
    slot_index = jnp.arange(others, dtype=jnp.int32)
    larger = floor_count[:, None] + (slot_index[None, :] < remain[:, None]).astype(jnp.int32)
    row_keys = jax.random.split(order_key, shards)

    def permute_row(row_key):
        return jax.random.permutation(row_key, others)
    orders = jax.vmap(permute_row)(row_keys)
    mixed = jnp.take_along_axis(larger, orders, axis=1)
    place = jax.random.randint(place_key, (shards,), 0, others + 1).astype(jnp.int32)
    token_slot = jnp.arange(TOK_DEV, dtype=jnp.int32)[None, :]
    is_single = (token_slot >= place[:, None]) & (token_slot < place[:, None] + single)
    rank = jnp.where(token_slot < place[:, None], token_slot, token_slot - single)
    rank = jnp.clip(rank, 0, others - 1).astype(jnp.int32)
    multi = jnp.take_along_axis(mixed, rank, axis=1)
    counts = jnp.where(is_single, 1, multi)
    return counts.reshape(TOKENS).astype(jnp.int32)


def draw_token_atoms(key, part):
    return shared_counts(key)


def draw_atom_token(key, part):
    counts = shared_counts(key)
    return jnp.repeat(jnp.arange(TOKENS, dtype=jnp.int32), counts, total_repeat_length=ATOMS).astype(jnp.int32)


def touch_ends(values, stream_key, low, high):
    index_at = [jax.random.randint(jax.random.fold_in(stream_key, axis), (), 0, length) for axis, length in enumerate(values.shape)]
    main_axis = values.shape.index(max(values.shape))
    beside = index_at[:main_axis] + [(index_at[main_axis] + 1) % values.shape[main_axis]] + index_at[main_axis + 1:]
    return values.at[tuple(index_at)].set(low).at[tuple(beside)].set(high)


def levels(key, dims, cuts, low, largest):
    loudness = 1.0
    for dim, blocks in cuts:
        draws = jax.random.uniform(jax.random.fold_in(jax.random.fold_in(key, 6), dim), (blocks,), jnp.float32, low / len(cuts), largest / len(cuts))
        loudness = loudness * jnp.repeat(jnp.exp(draws), dims[dim] // blocks).reshape((-1,) + (1,) * (len(dims) - 1 - dim))
    return loudness


def normal_values(rng, dims, scale, reach, cuts=(), held_as=jnp.bfloat16):
    array = scale * jax.random.normal(rng, dims, jnp.float32)
    if cuts:
        array = array * levels(rng, dims, cuts, -0.22, 0.18)
    return jnp.clip(array, -reach, reach).astype(held_as)


def setup_inputs(seed: int = 0, part: int = 0) -> dict:
    key_list = jax.random.split(jax.random.key(seed), 15)
    part_splits = jax.random.split(jax.random.fold_in(key_list[14], part), 15)
    return {
        "atom_single": normal_values(part_splits[0], (ATOMS, C), 1.0, 6.0, ((0, 16),)),
        "atom_token": draw_atom_token(jax.random.fold_in(jax.random.fold_in(key_list[14], part), 71), part),
        "token_atoms": draw_token_atoms(jax.random.fold_in(jax.random.fold_in(key_list[14], part), 71), part),
        "window_offset": touch_ends(jax.random.randint(part_splits[3], (ATOMS // QB,), 0, HALO + 1), jax.random.fold_in(part_splits[3], 1), 0, HALO).astype(jnp.int32),
        "token_pair": normal_values(part_splits[4], (TOKENS, BANDW, CZ), 1.0, 6.0, ((0, 16),)),
        "w_zpair": normal_values(key_list[5], (CZ, CP), CZ ** -0.5, 0.5),
        "w_single": normal_values(key_list[6], (2, C, CP), C ** -0.5, 0.5),
        "w_pair_mlp": normal_values(key_list[7], (3, CP, CP), CP ** -0.5, 1.5),
        "w_bias": normal_values(key_list[8], (BLOCKS, CP, HEADS), CP ** -0.5, 1.5),
        "w_attn": normal_values(key_list[9], (BLOCKS, 4, C, C), C ** -0.5, 0.5),
        "w_out": normal_values(key_list[10], (BLOCKS, C, C), C ** -0.5, 0.5),
        "w_trans_in": normal_values(key_list[11], (BLOCKS, 2, C, TH), C ** -0.5, 0.5),
        "w_trans_out": normal_values(key_list[12], (BLOCKS, TH, C), TH ** -0.5, 0.375),
        "w_token": normal_values(key_list[13], (C, CT), C ** -0.5, 0.5),
    }


EPSILON = 1e-05

def normalize(values, axis):
    centre = lax.optimization_barrier(jnp.mean(values, axis=axis, keepdims=True))
    shifted = values - centre
    spread = lax.optimization_barrier(jnp.mean(shifted * shifted, axis=axis, keepdims=True))
    return shifted * lax.rsqrt(spread + EPSILON)

def reference(atom_single, atom_token, token_atoms, window_offset, token_pair, w_zpair, w_single, w_pair_mlp, w_bias, w_attn, w_out, w_trans_in, w_trans_out, w_token):
    windows = ATOMS // QB
    per_shard = ATOM_DEV // QB
    high = lax.Precision.HIGHEST
    w_zpair_f = w_zpair.astype(jnp.float32)

    def project_block(rows):
        normed_rows = normalize(rows.astype(jnp.float32), 2).astype(jnp.bfloat16)
        return jnp.einsum('twc,ce->twe', normed_rows.astype(jnp.float32), w_zpair_f).astype(jnp.bfloat16)
    token_proj = lax.map(project_block, token_pair.reshape(TOKENS // TOK_DEV, TOK_DEV, BANDW, CZ)).reshape(TOKENS, BANDW, CP)
    relu_single = jnp.maximum(atom_single, jnp.zeros((), atom_single.dtype))
    query_term = jnp.dot(relu_single, w_single[0], preferred_element_type=jnp.float32)
    key_term = jnp.dot(relu_single, w_single[1], preferred_element_type=jnp.float32).astype(jnp.bfloat16)
    offsets = jnp.arange(KW, dtype=jnp.int32)
    starts = QB * jnp.arange(windows, dtype=jnp.int32) - HALO + window_offset.astype(jnp.int32)
    key_index = starts[:, None] + offsets[None, :]
    inside = (key_index >= 0) & (key_index < ATOMS)
    safe_index = jnp.clip(key_index, 0, ATOMS - 1)
    valid = inside.astype(jnp.float32)
    key_tokens = jnp.where(inside, atom_token[safe_index], 0).astype(jnp.int32)
    key_side = jnp.where(inside[:, :, None], key_term[safe_index], jnp.zeros((), key_term.dtype))
    query_tokens = atom_token.reshape(windows, QB)
    column = jnp.clip(key_tokens[:, None, :] - query_tokens[:, :, None] + BANDW // 2, 0, BANDW - 1).astype(jnp.int32)
    mlp_f = w_pair_mlp.astype(jnp.float32)
    bias_f = w_bias.astype(jnp.float32)

    def shard_bias(inputs):
        shard_tokens, shard_column, shard_query, shard_key = inputs
        gathered = token_proj[shard_tokens[:, :, None], shard_column]
        pair_start = gathered.astype(jnp.float32) + shard_query.reshape(per_shard, QB, 1, CP) + shard_key[:, None, :, :].astype(jnp.float32)
        first = jnp.einsum('nqke,ef->nqkf', jax.nn.relu(pair_start), mlp_f[0], precision=high)
        second = jnp.einsum('nqke,ef->nqkf', jax.nn.relu(first), mlp_f[1], precision=high)
        third = jnp.einsum('nqke,ef->nqkf', jax.nn.relu(second), mlp_f[2], precision=high)
        pair = pair_start + third
        return jnp.einsum('nqke,leh->lhnqk', normalize(pair, 3), bias_f, precision=high)
    stacked = lax.map(shard_bias, (query_tokens.reshape(SHARDS, per_shard, QB), column.reshape(SHARDS, per_shard, QB, KW), query_term.reshape(SHARDS, per_shard * QB, CP), key_side.reshape(SHARDS, per_shard, KW, CP)))
    bias = jnp.transpose(stacked, (1, 2, 0, 3, 4, 5)).reshape(BLOCKS, HEADS, windows, QB, KW)
    act = atom_single.astype(jnp.float32)
    for layer_index in range(BLOCKS):
        normed = normalize(act, 1).astype(jnp.bfloat16)
        queries = jnp.dot(normed, w_attn[layer_index, 0], preferred_element_type=jnp.float32).astype(jnp.bfloat16)
        keys_all = jnp.dot(normed, w_attn[layer_index, 1], preferred_element_type=jnp.float32).astype(jnp.bfloat16)
        values_all = jnp.dot(normed, w_attn[layer_index, 2], preferred_element_type=jnp.float32).astype(jnp.bfloat16)
        gate_logit = jnp.dot(normed, w_attn[layer_index, 3], preferred_element_type=jnp.float32)
        window_keys = jnp.where(inside[:, :, None], keys_all[safe_index], jnp.zeros((), keys_all.dtype)).reshape(windows, KW, HEADS, HD)
        window_values = jnp.where(inside[:, :, None], values_all[safe_index], jnp.zeros((), values_all.dtype)).reshape(windows, KW, HEADS, HD)
        query_heads = queries.reshape(windows, QB, HEADS, HD)
        scores = jnp.einsum('nqhd,nkhd->hnqk', query_heads.astype(jnp.float32), window_keys.astype(jnp.float32)) / math.sqrt(HD) + bias[layer_index]
        weights = jnp.exp(scores) * valid[None, :, None, :]
        weights = (weights / lax.optimization_barrier(jnp.sum(weights, axis=3, keepdims=True))).astype(jnp.bfloat16)
        attended = jnp.einsum('hnqk,nkhd->nqhd', weights.astype(jnp.float32), window_values.astype(jnp.float32)).reshape(ATOMS, C)
        gated = (attended * jax.nn.sigmoid(gate_logit)).astype(jnp.bfloat16)
        act = act + jnp.dot(gated, w_out[layer_index], preferred_element_type=jnp.float32)
        normed_two = normalize(act, 1).astype(jnp.bfloat16)
        gate_part = jnp.dot(normed_two, w_trans_in[layer_index, 0], preferred_element_type=jnp.float32)
        up_part = jnp.dot(normed_two, w_trans_in[layer_index, 1], preferred_element_type=jnp.float32)
        hidden_units = (jax.nn.silu(gate_part) * up_part).astype(jnp.bfloat16)
        act = act + jnp.dot(hidden_units, w_trans_out[layer_index], preferred_element_type=jnp.float32)
    atom_out = act.astype(jnp.bfloat16)
    features = jax.nn.relu(jnp.dot(atom_out, w_token, preferred_element_type=jnp.float32))
    sums = jax.ops.segment_sum(features, atom_token, num_segments=TOKENS)
    token_single = (sums / token_atoms[:, None].astype(jnp.float32)).astype(jnp.bfloat16)
    return (token_single, atom_out)
```

```python
import functools
import math

import jax
import jax.numpy as jnp
from jax import lax
from jax.experimental import pallas as pl
from jax.experimental.pallas import tpu as pltpu
from jax.sharding import PartitionSpec as P

BLOCKS = 3
QB = 32
KW = 128
HALO = 96
LANES = 128
CHUNK = 3
EPSILON = 1e-05
RING = ("seq", "chan", "sub")
NT = (((1,), (1,)), ((), ()))
F32 = jnp.float32
BF16 = jnp.bfloat16


def dot(a, b):
    return jnp.dot(a, b, preferred_element_type=F32)


def dot_nt(a, b):
    return lax.dot_general(a, b, NT, preferred_element_type=F32)


def iota(shape, axis):
    return lax.broadcasted_iota(jnp.int32, shape, axis)


def shard_place():
    index, count = 0, 1
    for name in RING:
        index = index * lax.axis_size(name) + lax.axis_index(name)
        count = count * lax.axis_size(name)
    return index, count


def normalize(values, axis):
    centre = jnp.mean(values, axis=axis, keepdims=True)
    shifted = values - centre
    spread = jnp.mean(shifted * shifted, axis=axis, keepdims=True)
    return shifted * lax.rsqrt(spread + EPSILON)


def project_kernel(pair_ref, wz_ref, atom_ref, meta_ref, out_ref):
    rows, width = pair_ref.shape
    atoms = atom_ref.shape[0]
    channels = wz_ref.shape[1]
    eye = iota((width, width), 0) == iota((width, width), 1)
    centring = (eye.astype(F32) - 1.0 / width).astype(BF16)
    average = jnp.full((channels, width), 1.0 / width, BF16)
    wz_t = jnp.transpose(wz_ref[...].astype(F32)).astype(BF16)
    step = 512
    for first in range(0, rows, step):
        shifted = dot(pair_ref[first : first + step, :], centring)
        spread = dot_nt(average, (shifted * shifted).astype(BF16))
        projected = dot_nt(wz_t, shifted.astype(BF16))
        projected = (projected * lax.rsqrt(spread + EPSILON)).astype(BF16)
        for part in range(step // LANES):
            row = atoms + channels * ((first // LANES) + part)
            out_ref[row : row + channels, :] = projected[:, LANES * part : LANES * (part + 1)]
    out_ref[0:atoms, :] = atom_ref[...]
    row = atoms + channels * (rows // LANES)
    out_ref[row : row + 16, :] = meta_ref[...]


def spread_weight(weight_t, rows, ratio):
    side = weight_t.shape[1]
    cols = 256
    right = (iota((cols, side), 0) % side == iota((cols, side), 1)).astype(BF16)
    full = dot_nt(weight_t, right)
    same = (iota((rows, cols), 0) % ratio) == (iota((rows, cols), 1) // side)
    return jnp.where(same, full, 0.0).astype(BF16)


def main_kernel(
    own_ref,
    left_ref,
    right_ref,
    w_single_ref,
    w_mlp_ref,
    w_bias_ref,
    w_attn_ref,
    w_out_ref,
    w_in_ref,
    w_trans_out_ref,
    w_token_ref,
    token_out_ref,
    atom_out_ref,
    scalars_vmem,
    scalars,
    token_rows,
    key_terms,
    query_terms,
    tables,
    bias_ref,
    act_ref,
    query_ref,
    gate_ref,
    key_ref,
    value_ref,
    gated_ref,
    feature_ref,
    sem,
):
    index, count = shard_place()
    atoms, width = atom_out_ref.shape
    tokens = token_out_ref.shape[0]
    channels = w_mlp_ref.shape[1]
    heads = w_bias_ref.shape[2]
    head_size = width // heads
    tiles = atoms // LANES
    pairs = tokens // 2
    meta = atoms + channels * pairs
    first_valid = jnp.where(index == 0, atoms, 0)
    end_valid = jnp.where(index == count - 1, 2 * atoms, 3 * atoms)

    sides = (left_ref, own_ref, right_ref)
    shift_of = (-tokens, 0, tokens)
    number = iota((3 * tiles, LANES), 0) * LANES + iota((3 * tiles, LANES), 1)
    relative = jnp.concatenate(
        [ref[meta : meta + 16, :].astype(F32)[0:tiles] + s for ref, s in zip(sides, shift_of)],
        axis=0,
    )
    inside = (number >= first_valid) & (number < end_valid)
    relative = jnp.where(inside, relative, -64.0)
    relative_int = relative.astype(jnp.int32)
    metas = [ref[meta : meta + 16, :].astype(F32) for ref in sides]
    offset_lanes = atoms // QB
    offset_row = (
        metas[0][3:4]
        + pltpu.roll(metas[1][3:4], offset_lanes, 1)
        + pltpu.roll(metas[2][3:4], 2 * offset_lanes, 1)
    )
    scalars_vmem[0 : 3 * tiles, :] = jnp.clip(relative_int, 0, 3 * tokens - 1)
    scalars_vmem[3 * tiles : 3 * tiles + 1, :] = offset_row.astype(jnp.int32)
    copy = pltpu.make_async_copy(scalars_vmem, scalars, sem)
    copy.start()
    for tile in range(3 * tiles):
        token_rows[tile] = jnp.broadcast_to(relative_int[tile : tile + 1], (8, LANES))
    token_rows[3 * tiles] = jnp.zeros((8, LANES), jnp.int32)

    w_query_t = jnp.transpose(w_single_ref[0].astype(F32)).astype(BF16)
    w_key_t = jnp.transpose(w_single_ref[1].astype(F32)).astype(BF16)
    w_terms = jnp.concatenate([w_query_t, w_key_t], axis=0)
    for side, ref in enumerate(sides):
        for tile in range(tiles):
            rows = ref[tile * LANES : (tile + 1) * LANES, :]
            at = side * tiles + tile
            act_ref[at * LANES : (at + 1) * LANES, :] = rows.astype(F32)
            terms = dot_nt(w_terms, jnp.maximum(rows, jnp.zeros((), BF16)))
            query_terms[at] = terms[0:channels]
            key_terms[at] = terms[channels:].astype(BF16).astype(F32)
        for pair in range(pairs):
            row = atoms + channels * pair
            tables[side * pairs + pair] = ref[row : row + channels, :].astype(F32)
    key_terms[3 * tiles] = jnp.zeros((channels, LANES), F32)

    big = 256
    group = big // channels
    select = (iota((big, channels), 0) % channels == iota((big, channels), 1)).astype(BF16)
    same_block = (iota((big, big), 0) // channels) == (iota((big, big), 1) // channels)
    mlp = []
    for layer in range(3):
        by_row = dot_nt(select, w_mlp_ref[layer]).astype(BF16)
        mlp.append(jnp.where(same_block, dot_nt(by_row, select), 0.0).astype(BF16))
    per_block = heads * group
    pick_head = (iota((per_block, heads), 0) // group == iota((per_block, heads), 1)).astype(BF16)
    same_query = (iota((per_block, big), 0) % group) == (iota((per_block, big), 1) // channels)
    bias_parts = []
    for layer in range(BLOCKS):
        by_row = dot_nt(pick_head, w_bias_ref[layer]).astype(BF16)
        bias_parts.append(jnp.where(same_query, dot_nt(by_row, select), 0.0).astype(BF16))
    bias_weight = jnp.concatenate(bias_parts, axis=0)

    copy.wait()
    lane = iota((channels, LANES), 1)
    lane8 = iota((8, LANES), 1)
    first_query = 2 * HALO
    window_count = (atoms + HALO + 4 * HALO) // QB

    def key_start(n):
        return HALO + QB * n + scalars[3 * tiles, n + offset_lanes - 2 * HALO // QB]

    def bias_window(n, carry):
        query = first_query + QB * n
        query_tile = query // LANES
        query_lane = query % LANES
        start = key_start(n)
        tile = start // LANES
        shift = start % LANES
        back = LANES - shift
        key_tokens = pltpu.roll(
            jnp.where(lane8 >= shift, token_rows[tile], token_rows[tile + 1]), back, 1
        )
        key_side = pltpu.roll(
            jnp.where(lane >= shift, key_terms[tile], key_terms[tile + 1]), back, 1
        )
        query_side = pltpu.roll(query_terms[query_tile], LANES - query_lane, 1)
        pieces = []
        for i in range(QB):
            token = scalars[query_tile, query_lane + i]
            low = (token & 1) * (LANES // 2)
            column = jnp.clip(
                key_tokens + (low + LANES // 4 - token), low, low + LANES // 2 - 1
            )
            table = tables[token >> 1]
            gathered = [
                jnp.take_along_axis(
                    table[8 * g : 8 * (g + 1)], column, axis=1, mode="promise_in_bounds"
                )
                for g in range(channels // 8)
            ]
            pieces.append(
                jnp.concatenate(gathered, axis=0) + key_side + query_side[:, i : i + 1]
            )
        half = QB // 2
        start_pair = jnp.concatenate(
            [jnp.concatenate(pieces[:half], axis=0), jnp.concatenate(pieces[half:], axis=0)],
            axis=1,
        )
        hidden = start_pair
        for layer in range(3):
            hidden = dot(mlp[layer], jnp.maximum(hidden, 0.0).astype(BF16))
        pair = (start_pair + hidden).reshape(group, channels, big)
        normed = normalize(pair, 1).reshape(big, big).astype(BF16)
        bias = dot(bias_weight, normed)
        for layer in range(BLOCKS):
            part = bias[layer * per_block : (layer + 1) * per_block]
            bias_ref[n, layer, 0:per_block, :] = part[:, 0:LANES]
            bias_ref[n, layer, per_block : 2 * per_block, :] = part[:, LANES:]
        return carry

    lax.fori_loop(0, window_count, bias_window, 0)

    head_of_lane = iota((QB // 2, width), 1) // head_size
    scale = 1.0 / math.sqrt(head_size)

    def project(layer, first, rows, chunk):
        for row in range(first, first + rows, chunk):
            where = slice(row, row + chunk)
            normed = normalize(act_ref[where, :], 1).astype(BF16)
            number = iota((chunk, width), 0) + row
            held = (number >= first_valid) & (number < end_valid)
            query_ref[where, :] = dot(normed, w_attn_ref[layer, 0]) * scale
            key_ref[where, :] = jnp.where(held, dot(normed, w_attn_ref[layer, 1]), 0.0)
            value_ref[where, :] = jnp.where(held, dot(normed, w_attn_ref[layer, 2]), 0.0)
            gate_ref[where, :] = dot(normed, w_attn_ref[layer, 3])

    def attend(layer, n):
        query = pl.multiple_of(first_query + QB * n, QB)
        start = key_start(n)
        q = query_ref[pl.ds(query, QB), :]
        k = key_ref[pl.ds(start, KW), :].astype(BF16)
        v = value_ref[pl.ds(start, KW), :].astype(BF16)
        number = iota((KW, LANES), 0) + start
        held = jnp.where((number >= first_valid) & (number < end_valid), 1.0, 0.0).astype(BF16)
        blocks = []
        for half in range(2):
            part = q[half * QB // 2 : (half + 1) * QB // 2]
            for h in range(heads):
                blocks.append(jnp.where(head_of_lane == h, part, 0.0).astype(BF16))
        scores = dot_nt(jnp.concatenate(blocks, axis=0), k) + bias_ref[n, layer]
        weights = jnp.exp(scores).astype(BF16)
        sums = dot(weights, jnp.concatenate([v, held], axis=1))
        halves = []
        for half in range(2):
            base = half * per_block
            total = sums[base : base + group]
            for h in range(1, heads):
                row = base + h * group
                chosen = jnp.concatenate([head_of_lane == h] * 2, axis=1)
                total = jnp.where(chosen, sums[row : row + group], total)
            halves.append(total[:, :LANES] / total[:, LANES:])
        attended = jnp.concatenate(halves, axis=0)
        gated_ref[pl.ds(query, QB), :] = attended * jax.nn.sigmoid(
            gate_ref[pl.ds(query, QB), :]
        )

    def dense(layer, first, rows, chunk):
        for row in range(first, first + rows, chunk):
            where = slice(row, row + chunk)
            number = iota((chunk, width), 0) + row
            held = (number >= first_valid) & (number < end_valid)
            act = act_ref[where, :] + dot(gated_ref[where, :].astype(BF16), w_out_ref[layer])
            act = jnp.where(held, act, 0.0)
            normed = normalize(act, 1).astype(BF16)
            gate_part = dot(normed, w_in_ref[layer, 0])
            up_part = dot(normed, w_in_ref[layer, 1])
            hidden = (gate_part / (1.0 + jnp.exp(-gate_part)) * up_part).astype(BF16)
            act_ref[where, :] = act + dot(hidden, w_trans_out_ref[layer])

    chunk_of = (288, 336, 240)
    for layer in range(BLOCKS):
        first_window = layer * HALO // QB
        last_window = window_count - layer * HALO // QB
        query_first = first_query + QB * first_window
        query_rows = QB * (last_window - first_window)
        key_first = query_first - HALO
        key_rows = query_rows + 2 * HALO
        project(layer, key_first, key_rows, key_rows // 3)

        def attend_step(step, carry):
            for w in range(CHUNK):
                attend(layer, first_window + step * CHUNK + w)
            return carry

        lax.fori_loop(0, (last_window - first_window) // CHUNK, attend_step, 0)
        dense(layer, query_first, query_rows, chunk_of[layer])

    atom_out_ref[...] = act_ref[atoms : 2 * atoms, :].astype(BF16)
    reach = atoms + LANES
    feature_ref[atoms + HALO : reach, :] = jnp.zeros_like(feature_ref[atoms + HALO : reach, :])
    for row in range(0, atoms + HALO, 160):
        rows = act_ref[atoms + row : atoms + row + 160, :].astype(BF16)
        features = jnp.maximum(dot(rows, w_token_ref[...]), 0.0)
        feature_ref[row : row + 160, :] = features.astype(BF16)
    slot = iota((tokens, LANES), 0) + tokens
    member = jnp.concatenate(
        [
            (slot == relative_int[tile : tile + 1]).astype(F32)
            for tile in range(tiles, 2 * tiles + 1)
        ],
        axis=1,
    ).astype(BF16)
    sums = dot(member, feature_ref[...])
    diagonal = (iota((tokens, LANES), 0) == iota((tokens, LANES), 1)).astype(F32)
    atoms_of = jnp.sum(diagonal * metas[1][4:5], axis=1, keepdims=True)
    token_out_ref[...] = (sums / atoms_of).astype(BF16)


def shards(
    atom_single,
    atom_token,
    token_atoms,
    window_offset,
    token_pair,
    w_zpair,
    w_single,
    w_pair_mlp,
    w_bias,
    w_attn,
    w_out,
    w_trans_in,
    w_trans_out,
    w_token,
):
    index, count = shard_place()
    atoms, width = atom_single.shape
    tokens, band, depth = token_pair.shape
    channels = w_zpair.shape[1]
    tiles = atoms // LANES
    pairs = tokens * band // LANES
    payload_rows = atoms + channels * pairs + 16

    local = (atom_token - (index - 1) * tokens).reshape(tiles, LANES)
    meta = jnp.concatenate(
        [
            local,
            jnp.pad(window_offset, (0, LANES - window_offset.shape[0]))[None],
            jnp.pad(token_atoms, (0, LANES - tokens))[None],
            jnp.zeros((16 - tiles - 2, LANES), jnp.int32),
        ],
        axis=0,
    ).astype(BF16)
    vmem = pl.BlockSpec(memory_space=pltpu.VMEM)
    payload = pl.pallas_call(
        project_kernel,
        out_shape=jax.ShapeDtypeStruct((payload_rows, width), BF16),
        in_specs=[vmem] * 4,
        out_specs=vmem,
        name="project",
    )(token_pair.reshape(tokens * band, depth), w_zpair, atom_single, meta)
    up = [(i, i + 1) for i in range(count - 1)]
    down = [(i + 1, i) for i in range(count - 1)]
    left = lax.ppermute(payload, RING, up)
    right = lax.ppermute(payload, RING, down)

    reach = 3 * atoms
    windows = (atoms + 5 * HALO) // QB
    heads = w_bias.shape[2]
    channels_out = w_token.shape[1]
    token_single, atom_out = pl.pallas_call(
        main_kernel,
        out_shape=(
            jax.ShapeDtypeStruct((tokens, channels_out), BF16),
            jax.ShapeDtypeStruct((atoms, width), BF16),
        ),
        in_specs=[vmem] * 11,
        out_specs=(vmem, vmem),
        scratch_shapes=[
            pltpu.VMEM((16, LANES), jnp.int32),
            pltpu.SMEM((16, LANES), jnp.int32),
            pltpu.VMEM((3 * tiles + 1, 8, LANES), jnp.int32),
            pltpu.VMEM((3 * tiles + 1, channels, LANES), F32),
            pltpu.VMEM((3 * tiles, channels, LANES), F32),
            pltpu.VMEM((3 * pairs, channels, LANES), F32),
            pltpu.VMEM((windows, BLOCKS, heads * QB, KW), F32),
            pltpu.VMEM((reach, width), F32),
            pltpu.VMEM((reach, width), F32),
            pltpu.VMEM((reach, width), F32),
            pltpu.VMEM((reach, width), F32),
            pltpu.VMEM((reach, width), F32),
            pltpu.VMEM((reach, width), F32),
            pltpu.VMEM((atoms + LANES, channels_out), BF16),
            pltpu.SemaphoreType.DMA,
        ],
        compiler_params=pltpu.CompilerParams(vmem_limit_bytes=48 * 2**20),
        name="encode",
    )(
        payload,
        left,
        right,
        w_single,
        w_pair_mlp,
        w_bias,
        w_attn,
        w_out,
        w_trans_in,
        w_trans_out,
        w_token,
    )
    return token_single, atom_out


def solution(mesh):
    split = ("group", "seq", "chan", "sub")
    in_specs = (
        P(split, None),
        P(split),
        P(split),
        P(split),
        P(split, None, None),
        P(),
        P(),
        P(),
        P(),
        P(),
        P(),
        P(),
        P(),
        P(),
    )
    out_specs = (P(split, None), P(split, None))
    return jax.shard_map(shards, mesh=mesh, in_specs=in_specs, out_specs=out_specs, check_vma=False)
```

```python
import math

import jax
import jax.numpy as jnp
from jax import lax
from jax.experimental import pallas as pl
from jax.experimental.pallas import tpu as pltpu
from jax.sharding import PartitionSpec as P

BLOCKS = 3
QB = 32
KW = 128
HALO = 96
LANES = 128
PAIR_DEPTH = 6
PAIR_SLOTS = 4
PAIR_UNROLL = 3
EPSILON = 1e-05
RING = ("seq", "chan", "sub")
NT = (((1,), (1,)), ((), ()))
F32 = jnp.float32
BF16 = jnp.bfloat16


def dot(a, b):
    return jnp.dot(a, b, preferred_element_type=F32)


def dot_nt(a, b):
    return lax.dot_general(a, b, NT, preferred_element_type=F32)


def iota(shape, axis):
    return lax.broadcasted_iota(jnp.int32, shape, axis)


def shard_place():
    index, count = 0, 1
    for name in RING:
        index = index * lax.axis_size(name) + lax.axis_index(name)
        count = count * lax.axis_size(name)
    return index, count


def normalize(values, axis):
    centre = jnp.mean(values, axis=axis, keepdims=True)
    shifted = values - centre
    spread = jnp.mean(shifted * shifted, axis=axis, keepdims=True)
    return shifted * lax.rsqrt(spread + EPSILON)


def project_kernel(pair_ref, wz_ref, atom_ref, meta_ref, out_ref):
    rows, width = pair_ref.shape
    atoms = atom_ref.shape[0]
    channels = wz_ref.shape[0]
    eye = iota((width, width), 0) == iota((width, width), 1)
    centring = (eye.astype(F32) - 1.0 / width).astype(BF16)
    average = jnp.full((channels, width), 1.0 / width, BF16)
    step = 512
    for first in range(0, rows, step):
        shifted = dot(pair_ref[first : first + step, :], centring)
        spread = dot_nt(average, (shifted * shifted).astype(BF16))
        projected = dot_nt(wz_ref[...], shifted.astype(BF16))
        projected = (projected * lax.rsqrt(spread + EPSILON)).astype(BF16)
        for part in range(step // LANES):
            row = atoms + channels * ((first // LANES) + part)
            out_ref[row : row + channels, :] = projected[:, LANES * part : LANES * (part + 1)]
    out_ref[0:atoms, :] = atom_ref[...]
    row = atoms + channels * (rows // LANES)
    out_ref[row : row + 16, :] = meta_ref[...]


def main_kernel(
    own_ref,
    left_ref,
    right_ref,
    w_single_ref,
    w_mlp_ref,
    w_bias_ref,
    w_attn_ref,
    w_out_ref,
    w_in_ref,
    w_trans_out_ref,
    w_token_ref,
    token_out_ref,
    atom_out_ref,
    scalars_vmem,
    scalars,
    token_rows,
    key_terms,
    token_shift,
    token_base,
    table_rows,
    band_ref,
    side_ref,
    column_ref,
    start_ref,
    pair_ref,
    first_ref,
    second_ref,
    third_ref,
    normed_ref,
    left_terms,
    right_terms,
    mlp_ref,
    bias_weight_ref,
    bias_ref,
    act_ref,
    held_ref,
    query_ref,
    gate_ref,
    key_ref,
    value_ref,
    gated_ref,
    feature_ref,
    sem,
):
    index, count = shard_place()
    atoms, width = atom_out_ref.shape
    tokens = token_out_ref.shape[0]
    channels = w_mlp_ref.shape[1]
    heads = w_bias_ref.shape[1]
    head_size = width // heads
    tiles = atoms // LANES
    pairs = tokens // 2
    meta = atoms + channels * pairs
    first_valid = jnp.where(index == 0, atoms, 0)
    end_valid = jnp.where(index == count - 1, 2 * atoms, 3 * atoms)
    first_query = 2 * HALO
    window_count = (atoms + HALO + 4 * HALO) // QB
    query_end = first_query + QB * window_count

    sides = (left_ref, own_ref, right_ref)
    metas = [ref[meta : meta + 16, :].astype(F32) for ref in sides]
    number = iota((3 * tiles, LANES), 0) * LANES + iota((3 * tiles, LANES), 1)
    relative = jnp.concatenate(
        [m[0:tiles] + s for m, s in zip(metas, (-tokens, 0, tokens))], axis=0
    )
    inside = (number >= first_valid) & (number < end_valid)
    relative = jnp.where(inside, relative, -64.0)
    relative_int = relative.astype(jnp.int32)
    offset_lanes = atoms // QB
    offset_row = (
        metas[0][3:4]
        + pltpu.roll(metas[1][3:4], offset_lanes, 1)
        + pltpu.roll(metas[2][3:4], 2 * offset_lanes, 1)
    )
    scalars_vmem[...] = jnp.broadcast_to(offset_row, (8, LANES)).astype(jnp.int32)
    copy = pltpu.make_async_copy(scalars_vmem, scalars, sem)
    copy.start()
    for tile in range(3 * tiles):
        token_rows[tile] = jnp.broadcast_to(relative_int[tile : tile + 1], (8, LANES))
    token_rows[3 * tiles] = jnp.zeros((8, LANES), jnp.int32)

    big = 256
    group = big // channels
    select = (iota((big, channels), 0) // group == iota((big, channels), 1)).astype(BF16)
    same_query = (iota((big, big), 0) % group) == (iota((big, big), 1) % group)
    for layer in range(3):
        by_row = dot_nt(select, w_mlp_ref[layer]).astype(BF16)
        mlp_ref[layer] = jnp.where(same_query, dot_nt(by_row, select), 0.0).astype(BF16)
    per_block = heads * group
    pick_head = (iota((per_block, heads), 0) // group == iota((per_block, heads), 1)).astype(BF16)
    for layer in range(BLOCKS):
        by_row = dot(pick_head, w_bias_ref[layer]).astype(BF16)
        bias_weight_ref[layer * per_block : (layer + 1) * per_block, :] = jnp.where(
            same_query[0:per_block], dot_nt(by_row, select), 0.0
        ).astype(BF16)

    eye = iota((LANES, LANES), 0) == iota((LANES, LANES), 1)
    ones = jnp.ones((LANES, LANES), BF16)
    for side, ref in enumerate(sides):
        for tile in range(tiles):
            rows = ref[tile * LANES : (tile + 1) * LANES, :]
            at = side * tiles + tile
            where = slice(at * LANES, (at + 1) * LANES)
            act_ref[where, :] = rows.astype(F32)
            held_ref[where, :] = (
                (iota((LANES, LANES), 0) + at * LANES >= first_valid)
                & (iota((LANES, LANES), 0) + at * LANES < end_valid)
            ).astype(F32)
            relu = jnp.maximum(rows, jnp.zeros((), BF16))
            key_terms[at] = dot_nt(w_single_ref[1], relu).astype(BF16).astype(F32)
            column = dot(jnp.where(eye, relative[at : at + 1], 0.0).astype(BF16), ones)
            column = column.astype(jnp.int32)
            base = (column & 1) * (LANES // 2)
            token_base[where, :] = base
            token_shift[where, :] = LANES // 4 - column
        for pair in range(pairs):
            row = atoms + channels * pair
            to = (side * pairs + pair) * channels
            table_rows[to : to + channels, :] = ref[row : row + channels, :].astype(F32)
    key_terms[3 * tiles] = jnp.zeros((channels, LANES), F32)

    w_query = jnp.transpose(w_single_ref[0].astype(F32))
    for tile in range(first_query // LANES, -(-query_end // LANES)):
        where = slice(tile * LANES, (tile + 1) * LANES)
        token = LANES // 4 - token_shift[where, :]
        hit = ((token >> 1) == iota((LANES, LANES), 1)).astype(F32).astype(BF16)
        left_terms[where, 0:LANES] = hit
        left_terms[where, LANES:] = jnp.maximum(act_ref[where, :], 0.0).astype(BF16)
    padded = -(-3 * pairs // 16) * 16
    for c in range(channels):
        at = slice(c % 2 * LANES, (c % 2 + 1) * LANES)
        rows = [
            table_rows[pl.ds(8 * channels * g + c, 8, stride=channels), :]
            for g in range(3 * pairs // 8)
        ]
        rows.append(jnp.zeros((padded - 3 * pairs, LANES), F32))
        right_terms[c // 2, 0:padded, at] = jnp.concatenate(rows, axis=0).astype(BF16)
        right_terms[c // 2, padded:LANES, at] = jnp.zeros((LANES - padded, LANES), BF16)
        right_terms[c // 2, LANES:, at] = jnp.broadcast_to(
            w_query[:, c : c + 1], (width, LANES)
        ).astype(BF16)

    def band_step(step, carry):
        for c in range(2):
            band = dot(left_terms[first_query:query_end, :], right_terms[2 * step + c])
            for d in range(2):
                at = slice(d * LANES, (d + 1) * LANES)
                band_ref[4 * step + 2 * c + d, first_query:query_end, :] = band[:, at]
        return carry

    lax.fori_loop(0, channels // 4, band_step, 0)

    copy.wait()
    lane = iota((channels, LANES), 1)
    lane8 = iota((8, LANES), 1)
    log2e = math.log2(math.e)

    def key_start(n):
        return HALO + QB * n + scalars[0, n + offset_lanes - 2 * HALO // QB]

    def window_of(step, behind):
        return jnp.clip(step - behind, 0, window_count - 1)

    def column_stage(step):
        n = window_of(step, 0)
        query = pl.multiple_of(first_query + QB * n, QB)
        start = key_start(n)
        tile = start // LANES
        shift = start % LANES
        back = LANES - shift
        key_tokens = pltpu.roll(
            jnp.where(lane8 >= shift, token_rows[tile], token_rows[tile + 1]), back, 1
        )
        side_ref[...] = pltpu.roll(
            jnp.where(lane >= shift, key_terms[tile], key_terms[tile + 1]), back, 1
        )
        for g in range(QB // 8):
            rows = pl.ds(query + 8 * g, 8)
            column_ref[8 * g : 8 * g + 8, :] = (
                jnp.clip(key_tokens + token_shift[rows, :], 0, LANES // 2 - 1)
                + token_base[rows, :]
            )

    def start_stage(step):
        query = pl.multiple_of(first_query + QB * window_of(step, 1), QB)
        slot = step % PAIR_SLOTS
        for half in range(2):
            at = slice(half * LANES, (half + 1) * LANES)
            pieces = [[] for _ in range(channels)]
            for g in range(half * group // 8, (half + 1) * group // 8):
                column = column_ref[8 * g : 8 * g + 8, :]
                rows = pl.ds(query + 8 * g, 8)
                for e in range(channels):
                    pieces[e].append(
                        jnp.take_along_axis(
                            band_ref[e, rows, :], column, axis=1, mode="promise_in_bounds"
                        )
                        + jnp.broadcast_to(side_ref[e : e + 1, :], (8, LANES))
                    )
            for e in range(channels):
                piece = jnp.concatenate(pieces[e], axis=0)
                start_ref[slot, e * group : (e + 1) * group, at] = piece
                first_ref[e * group : (e + 1) * group, at] = jnp.maximum(
                    piece.astype(BF16), jnp.zeros((), BF16)
                )

    def hidden_stage(layer, from_ref, to_ref):
        hidden = dot(mlp_ref[layer], from_ref[...]).astype(BF16)
        to_ref[...] = jnp.maximum(hidden, jnp.zeros((), BF16))

    def sum_stage(step):
        pair_ref[...] = start_ref[(step + 1) % PAIR_SLOTS] + dot(mlp_ref[2], third_ref[...])

    def norm_stage():
        for half in range(2):
            at = slice(half * LANES, (half + 1) * LANES)
            pair = pair_ref[:, at].reshape(channels, group, LANES)
            shifted = pair - jnp.mean(pair, axis=0, keepdims=True)
            spread = jnp.mean(shifted * shifted, axis=0, keepdims=True)
            normed = shifted * (lax.rsqrt(spread + EPSILON) * log2e)
            normed_ref[:, at] = normed.reshape(big, LANES).astype(BF16)

    def bias_stage(step):
        n = window_of(step, PAIR_DEPTH)
        bias = dot(bias_weight_ref[...], normed_ref[...])
        for layer in range(BLOCKS):
            part = bias[layer * per_block : (layer + 1) * per_block]
            bias_ref[n, layer, 0:per_block, :] = part[:, 0:LANES]
            bias_ref[n, layer, per_block : 2 * per_block, :] = part[:, LANES:]

    def pair_step(outer, carry):
        for inner in range(PAIR_UNROLL):
            step = outer * PAIR_UNROLL + inner
            bias_stage(step)
            norm_stage()
            sum_stage(step)
            hidden_stage(1, second_ref, third_ref)
            hidden_stage(0, first_ref, second_ref)
            start_stage(step)
            column_stage(step)
        return carry

    lax.fori_loop(0, -(-(window_count + PAIR_DEPTH) // PAIR_UNROLL), pair_step, 0)

    head_of_lane = iota((QB // 2, width), 1) // head_size
    scale = log2e / math.sqrt(head_size)

    def project(layer, first, rows, chunk):
        w_first = jnp.concatenate([w_attn_ref[layer, 0], w_attn_ref[layer, 1]], axis=1)
        w_second = jnp.concatenate([w_attn_ref[layer, 2], w_attn_ref[layer, 3]], axis=1)
        for row in range(first, first + rows, chunk):
            where = slice(row, row + chunk)
            normed = normalize(act_ref[where, :], 1).astype(BF16)
            held = held_ref[where, :] > 0.0
            both = dot(normed, w_first)
            query_ref[where, :] = (both[:, :width] * scale).astype(BF16)
            key_ref[where, :] = jnp.where(held, both[:, width:], 0.0)
            both = dot(normed, w_second)
            value_ref[where, :] = jnp.where(held, both[:, :width], 0.0)
            gate_ref[where, :] = jax.nn.sigmoid(both[:, width:])

    def attend(layer, n):
        query = pl.multiple_of(first_query + QB * n, QB)
        start = key_start(n)
        q = query_ref[pl.ds(query, QB), :]
        k = key_ref[pl.ds(start, KW), :].astype(BF16)
        v = jnp.concatenate(
            [value_ref[pl.ds(start, KW), :], held_ref[pl.ds(start, KW), :]], axis=1
        ).astype(BF16)
        blocks = []
        for half in range(2):
            part = q[half * QB // 2 : (half + 1) * QB // 2]
            for h in range(heads):
                blocks.append(jnp.where(head_of_lane == h, part, jnp.zeros((), BF16)))
        scores = dot_nt(jnp.concatenate(blocks, axis=0), k) + bias_ref[n, layer]
        sums = dot(jnp.exp2(scores).astype(BF16), v)
        halves = []
        for half in range(2):
            base = half * per_block
            value = sums[base : base + group, :LANES]
            total = sums[base : base + group, LANES:]
            for h in range(1, heads):
                row = base + h * group
                value = jnp.where(head_of_lane == h, sums[row : row + group, :LANES], value)
                total = jnp.where(head_of_lane == h, sums[row : row + group, LANES:], total)
            halves.append(value / total)
        attended = jnp.concatenate(halves, axis=0)
        gated_ref[pl.ds(query, QB), :] = (attended * gate_ref[pl.ds(query, QB), :]).astype(BF16)

    def dense(layer, first, rows, chunk):
        for row in range(first, first + rows, chunk):
            where = slice(row, row + chunk)
            act = act_ref[where, :] + dot(gated_ref[where, :], w_out_ref[layer])
            act = jnp.where(held_ref[where, :] > 0.0, act, 0.0)
            normed = normalize(act, 1).astype(BF16)
            gate_part = dot(normed, w_in_ref[layer, 0])
            up_part = dot(normed, w_in_ref[layer, 1])
            hidden = (gate_part / (1.0 + jnp.exp(-gate_part)) * up_part).astype(BF16)
            act_ref[where, :] = act + dot(hidden, w_trans_out_ref[layer])

    chunk_of = (288, 336, 240)
    for layer in range(BLOCKS):
        first_window = layer * HALO // QB
        last_window = window_count - layer * HALO // QB
        windows = last_window - first_window
        query_first = first_query + QB * first_window
        query_rows = QB * windows
        key_first = query_first - HALO
        key_rows = query_rows + 2 * HALO
        project(layer, key_first, key_rows, key_rows // 3)

        def attend_step(step, carry):
            for w in range(windows // 3):
                attend(layer, first_window + step * (windows // 3) + w)
            return carry

        lax.fori_loop(0, 3, attend_step, 0)
        dense(layer, query_first, query_rows, chunk_of[layer])

    atom_out_ref[...] = act_ref[atoms : 2 * atoms, :].astype(BF16)
    reach = atoms + LANES
    feature_ref[atoms + HALO : reach, :] = jnp.zeros_like(feature_ref[atoms + HALO : reach, :])
    for row in range(0, atoms + HALO, 160):
        rows = act_ref[atoms + row : atoms + row + 160, :].astype(BF16)
        features = jnp.maximum(dot(rows, w_token_ref[...]), 0.0)
        feature_ref[row : row + 160, :] = features.astype(BF16)
    slot = iota((tokens, LANES), 0) + tokens
    member = jnp.concatenate(
        [
            (slot == relative_int[tile : tile + 1]).astype(F32)
            for tile in range(tiles, 2 * tiles + 1)
        ],
        axis=1,
    ).astype(BF16)
    sums = dot(member, feature_ref[...])
    diagonal = (iota((tokens, LANES), 0) == iota((tokens, LANES), 1)).astype(F32)
    atoms_of = jnp.sum(diagonal * metas[1][4:5], axis=1, keepdims=True)
    token_out_ref[...] = (sums / atoms_of).astype(BF16)


def shards(
    atom_single,
    atom_token,
    token_atoms,
    window_offset,
    token_pair,
    w_zpair,
    w_single,
    w_pair_mlp,
    w_bias,
    w_attn,
    w_out,
    w_trans_in,
    w_trans_out,
    w_token,
):
    index, count = shard_place()
    atoms, width = atom_single.shape
    tokens, band, depth = token_pair.shape
    channels = w_zpair.shape[1]
    tiles = atoms // LANES
    pairs = tokens * band // LANES
    payload_rows = atoms + channels * pairs + 16

    local = (atom_token - (index - 1) * tokens).reshape(tiles, LANES)
    meta = jnp.concatenate(
        [
            local,
            jnp.pad(window_offset, (0, LANES - window_offset.shape[0]))[None],
            jnp.pad(token_atoms, (0, LANES - tokens))[None],
            jnp.zeros((16 - tiles - 2, LANES), jnp.int32),
        ],
        axis=0,
    ).astype(BF16)
    vmem = pl.BlockSpec(memory_space=pltpu.VMEM)
    payload = pl.pallas_call(
        project_kernel,
        out_shape=jax.ShapeDtypeStruct((payload_rows, width), BF16),
        in_specs=[vmem] * 4,
        out_specs=vmem,
        name="project",
    )(token_pair.reshape(tokens * band, depth), jnp.swapaxes(w_zpair, 0, 1), atom_single, meta)
    up = [(i, i + 1) for i in range(count - 1)]
    down = [(i + 1, i) for i in range(count - 1)]
    left = lax.ppermute(payload, RING, up)
    right = lax.ppermute(payload, RING, down)

    reach = 3 * atoms
    windows = (atoms + 5 * HALO) // QB
    heads = w_bias.shape[2]
    channels_out = w_token.shape[1]
    token_single, atom_out = pl.pallas_call(
        main_kernel,
        out_shape=(
            jax.ShapeDtypeStruct((tokens, channels_out), BF16),
            jax.ShapeDtypeStruct((atoms, width), BF16),
        ),
        in_specs=[vmem] * 11,
        out_specs=(vmem, vmem),
        scratch_shapes=[
            pltpu.VMEM((8, LANES), jnp.int32),
            pltpu.SMEM((8, LANES), jnp.int32),
            pltpu.VMEM((3 * tiles + 1, 8, LANES), jnp.int32),
            pltpu.VMEM((3 * tiles + 1, channels, LANES), F32),
            pltpu.VMEM((reach, LANES), jnp.int32),
            pltpu.VMEM((reach, LANES), jnp.int32),
            pltpu.VMEM((3 * pairs * channels, LANES), F32),
            pltpu.VMEM((channels, reach, LANES), F32),
            pltpu.VMEM((channels, LANES), F32),
            pltpu.VMEM((QB, LANES), jnp.int32),
            pltpu.VMEM((PAIR_SLOTS, 256, 256), F32),
            pltpu.VMEM((256, 256), F32),
            pltpu.VMEM((256, 256), BF16),
            pltpu.VMEM((256, 256), BF16),
            pltpu.VMEM((256, 256), BF16),
            pltpu.VMEM((256, 256), BF16),
            pltpu.VMEM((reach, 256), BF16),
            pltpu.VMEM((channels // 2, 256, 256), BF16),
            pltpu.VMEM((3, 256, 256), BF16),
            pltpu.VMEM((BLOCKS * heads * 256 // channels, 256), BF16),
            pltpu.VMEM((windows, BLOCKS, heads * QB, KW), F32),
            pltpu.VMEM((reach, width), F32),
            pltpu.VMEM((reach, LANES), F32),
            pltpu.VMEM((reach, width), BF16),
            pltpu.VMEM((reach, width), F32),
            pltpu.VMEM((reach, width), F32),
            pltpu.VMEM((reach, width), F32),
            pltpu.VMEM((reach, width), BF16),
            pltpu.VMEM((atoms + LANES, channels_out), BF16),
            pltpu.SemaphoreType.DMA,
        ],
        compiler_params=pltpu.CompilerParams(vmem_limit_bytes=48 * 2**20),
        name="encode",
    )(
        payload,
        left,
        right,
        jnp.swapaxes(w_single, 1, 2),
        w_pair_mlp,
        jnp.swapaxes(w_bias, 1, 2),
        w_attn,
        w_out,
        w_trans_in,
        w_trans_out,
        w_token,
    )
    return token_single, atom_out


def solution(mesh):
    split = ("group", "seq", "chan", "sub")
    in_specs = (
        P(split, None),
        P(split),
        P(split),
        P(split),
        P(split, None, None),
        P(),
        P(),
        P(),
        P(),
        P(),
        P(),
        P(),
        P(),
        P(),
    )
    out_specs = (P(split, None), P(split, None))
    return jax.shard_map(shards, mesh=mesh, in_specs=in_specs, out_specs=out_specs, check_vma=False)
```

```python
import math

import jax
import jax.numpy as jnp
from jax import lax
from jax.experimental import pallas as pl
from jax.experimental.pallas import tpu as pltpu
from jax.sharding import PartitionSpec as P

BLOCKS = 3
QB = 32
KW = 128
HALO = 96
LANES = 128
PAIR_DEPTH = 4
PAIR_SLOTS = 4
PAIR_GROUP = 3
EPSILON = 1e-05
RING = ("seq", "chan", "sub")
NT = (((1,), (1,)), ((), ()))
F32 = jnp.float32
BF16 = jnp.bfloat16


def dot(a, b):
    return jnp.dot(a, b, preferred_element_type=F32)


def dot_nt(a, b):
    return lax.dot_general(a, b, NT, preferred_element_type=F32)


def iota(shape, axis):
    return lax.broadcasted_iota(jnp.int32, shape, axis)


def shard_place():
    index, count = 0, 1
    for name in RING:
        index = index * lax.axis_size(name) + lax.axis_index(name)
        count = count * lax.axis_size(name)
    return index, count


def normalize(values, axis):
    centre = jnp.mean(values, axis=axis, keepdims=True)
    shifted = values - centre
    spread = jnp.mean(shifted * shifted, axis=axis, keepdims=True)
    return shifted * lax.rsqrt(spread + EPSILON)


def project_kernel(
    pair_hbm,
    wz_hbm,
    atom_hbm,
    token_hbm,
    atoms_of_hbm,
    offset_hbm,
    out_hbm,
    pair_ref,
    wz_ref,
    token_ref,
    atoms_of_ref,
    offset_ref,
    band_ref,
    meta_ref,
    small_sems,
    in_sems,
    out_sems,
):
    rows, width = pair_ref.shape
    atoms = atom_hbm.shape[0]
    tokens = atoms_of_hbm.shape[0]
    channels = wz_hbm.shape[0]
    tiles = atoms // LANES
    parts = in_sems.shape[0]
    step = rows // parts
    band_step = channels * step // LANES
    meta = atoms + channels * rows // LANES

    loads = [
        pltpu.make_async_copy(
            pair_hbm.at[pl.ds(step * part, step)],
            pair_ref.at[pl.ds(step * part, step)],
            in_sems.at[part],
        )
        for part in range(parts)
    ]
    small = [
        pltpu.make_async_copy(wz_hbm, wz_ref, small_sems.at[0]),
        pltpu.make_async_copy(token_hbm, token_ref, small_sems.at[1]),
        pltpu.make_async_copy(atoms_of_hbm, atoms_of_ref, small_sems.at[2]),
        pltpu.make_async_copy(offset_hbm, offset_ref, small_sems.at[3]),
    ]
    atom_copy = pltpu.make_async_copy(atom_hbm, out_hbm.at[pl.ds(0, atoms)], out_sems.at[parts])
    loads[0].start()
    for copy in small + loads[1:]:
        copy.start()
    atom_copy.start()

    eye = iota((width, width), 0) == iota((width, width), 1)
    centring = (eye.astype(F32) - 1.0 / width).astype(BF16)
    average = jnp.full((channels, width), 1.0 / width, BF16)
    for copy in small:
        copy.wait()
    index, _ = shard_place()
    meta_ref[...] = jnp.zeros_like(meta_ref)
    base = (index - 1) * tokens
    for tile in range(tiles):
        local = token_ref[LANES * tile : LANES * (tile + 1)].reshape(1, LANES) - base
        meta_ref[tile : tile + 1, :] = local.astype(F32)
    meta_ref[tiles : tiles + 1, 0 : offset_ref.shape[0]] = (
        offset_ref[...].reshape(1, offset_ref.shape[0]).astype(F32)
    )
    meta_ref[tiles + 1 : tiles + 2, 0:tokens] = (
        atoms_of_ref[...].reshape(1, tokens).astype(F32)
    )
    band_ref[meta - atoms :, :] = meta_ref[...].astype(BF16)
    stores = []
    for part in range(parts):
        loads[part].wait()
        shifted = dot(pair_ref[step * part : step * (part + 1), :], centring)
        spread = dot_nt(average, (shifted * shifted).astype(BF16))
        projected = dot_nt(wz_ref[...], shifted.astype(BF16))
        projected = (projected * lax.rsqrt(spread + EPSILON)).astype(BF16)
        for tile in range(step // LANES):
            row = band_step * part + channels * tile
            band_ref[row : row + channels, :] = projected[:, LANES * tile : LANES * (tile + 1)]
        first, count = band_step * part, band_step + (16 if part == parts - 1 else 0)
        copy = pltpu.make_async_copy(
            band_ref.at[pl.ds(first, count)],
            out_hbm.at[pl.ds(atoms + first, count)],
            out_sems.at[part],
        )
        copy.start()
        stores.append(copy)
    for copy in stores:
        copy.wait()
    atom_copy.wait()


def main_kernel(
    own_hbm,
    near_hbm,
    far_hbm,
    w_single_hbm,
    w_mlp_hbm,
    w_bias_hbm,
    w_attn_hbm,
    w_out_hbm,
    w_in_hbm,
    w_trans_out_hbm,
    w_token_hbm,
    token_out_ref,
    atom_out_ref,
    payload_ref,
    w_single_ref,
    w_mlp_ref,
    w_bias_ref,
    w_attn_ref,
    w_out_ref,
    w_in_ref,
    w_trans_out_ref,
    w_token_ref,
    scalars_vmem,
    scalars,
    token_rows,
    key_terms,
    token_shift,
    token_base,
    table_rows,
    band_ref,
    side_ref,
    column_ref,
    start_ref,
    second_ref,
    third_ref,
    normed_ref,
    left_terms,
    right_terms,
    mlp_ref,
    bias_weight_ref,
    bias_ref,
    act_ref,
    held_ref,
    query_ref,
    gate_ref,
    key_ref,
    value_ref,
    gated_ref,
    feature_ref,
    sems,
    weight_sems,
):
    index, count = shard_place()
    atoms, width = atom_out_ref.shape
    tokens = token_out_ref.shape[0]
    channels = w_mlp_ref.shape[1]
    heads = w_bias_ref.shape[1]
    head_size = width // heads
    tiles = atoms // LANES
    pairs = tokens // 2
    meta = atoms + channels * pairs
    first_valid = jnp.where(index == 0, atoms, 0)
    end_valid = jnp.where(index == count - 1, 2 * atoms, 3 * atoms)
    first_query = 2 * HALO
    window_count = (atoms + HALO + 4 * HALO) // QB
    query_end = first_query + QB * window_count

    even = index % 2 == 0
    copies = [
        pltpu.make_async_copy(own_hbm, payload_ref.at[1], sems.at[0]),
        pltpu.make_async_copy(near_hbm, payload_ref.at[jnp.where(even, 2, 0)], sems.at[1]),
        pltpu.make_async_copy(far_hbm, payload_ref.at[jnp.where(even, 0, 2)], sems.at[2]),
    ]
    weight_copies = [
        pltpu.make_async_copy(source, target, weight_sems.at[i])
        for i, (source, target) in enumerate(
            (
                (w_mlp_hbm, w_mlp_ref),
                (w_bias_hbm, w_bias_ref),
                (w_single_hbm, w_single_ref),
                (w_attn_hbm, w_attn_ref),
                (w_out_hbm, w_out_ref),
                (w_in_hbm, w_in_ref),
                (w_trans_out_hbm, w_trans_out_ref),
                (w_token_hbm, w_token_ref),
            )
        )
    ]
    for copy in weight_copies[:3] + copies + weight_copies[3:]:
        copy.start()
    for copy in weight_copies[:3]:
        copy.wait()

    big = 256
    group = big // channels
    select = (iota((big, channels), 0) // group == iota((big, channels), 1)).astype(BF16)
    same_query = (iota((big, big), 0) % group) == (iota((big, big), 1) % group)
    for layer in range(3):
        by_row = dot_nt(select, w_mlp_ref[layer]).astype(BF16)
        mlp_ref[layer] = jnp.where(same_query, dot_nt(by_row, select), 0.0).astype(BF16)
    per_block = heads * group
    pick_head = (iota((per_block, heads), 0) // group == iota((per_block, heads), 1)).astype(BF16)
    for layer in range(BLOCKS):
        by_row = dot(pick_head, w_bias_ref[layer]).astype(BF16)
        bias_weight_ref[layer * per_block : (layer + 1) * per_block, :] = jnp.where(
            same_query[0:per_block], dot_nt(by_row, select), 0.0
        ).astype(BF16)

    for copy in copies:
        copy.wait()
    sides = tuple(payload_ref.at[side] for side in range(3))
    metas = [ref[meta : meta + 16, :].astype(F32) for ref in sides]
    number = iota((3 * tiles, LANES), 0) * LANES + iota((3 * tiles, LANES), 1)
    relative = jnp.concatenate(
        [m[0:tiles] + s for m, s in zip(metas, (-tokens, 0, tokens))], axis=0
    )
    inside = (number >= first_valid) & (number < end_valid)
    relative = jnp.where(inside, relative, -64.0)
    relative_int = relative.astype(jnp.int32)
    offset_lanes = atoms // QB
    offset_row = (
        metas[0][3:4]
        + pltpu.roll(metas[1][3:4], offset_lanes, 1)
        + pltpu.roll(metas[2][3:4], 2 * offset_lanes, 1)
    )
    scalars_vmem[...] = jnp.broadcast_to(offset_row, (8, LANES)).astype(jnp.int32)
    copy = pltpu.make_async_copy(scalars_vmem, scalars, sems.at[3])
    copy.start()
    for tile in range(3 * tiles):
        token_rows[tile] = jnp.broadcast_to(relative_int[tile : tile + 1], (8, LANES))
    token_rows[3 * tiles] = jnp.zeros((8, LANES), jnp.int32)

    eye = iota((LANES, LANES), 0) == iota((LANES, LANES), 1)
    ones = jnp.ones((LANES, LANES), BF16)
    for side, ref in enumerate(sides):
        for tile in range(tiles):
            rows = ref[tile * LANES : (tile + 1) * LANES, :]
            at = side * tiles + tile
            where = slice(at * LANES, (at + 1) * LANES)
            act_ref[where, :] = rows.astype(F32)
            held_ref[where, :] = (
                (iota((LANES, LANES), 0) + at * LANES >= first_valid)
                & (iota((LANES, LANES), 0) + at * LANES < end_valid)
            ).astype(F32)
            relu = jnp.maximum(rows, jnp.zeros((), BF16))
            key_terms[at] = dot_nt(w_single_ref[1], relu).astype(BF16).astype(F32)
            column = dot(jnp.where(eye, relative[at : at + 1], 0.0).astype(BF16), ones)
            column = column.astype(jnp.int32)
            base = (column & 1) * (LANES // 2)
            token_base[where, :] = base
            token_shift[where, :] = LANES // 4 - column
        for pair in range(pairs):
            row = atoms + channels * pair
            to = (side * pairs + pair) * channels
            table_rows[to : to + channels, :] = ref[row : row + channels, :].astype(F32)
    key_terms[3 * tiles] = jnp.zeros((channels, LANES), F32)

    w_query = jnp.transpose(w_single_ref[0].astype(F32))
    for tile in range(first_query // LANES, -(-query_end // LANES)):
        where = slice(tile * LANES, (tile + 1) * LANES)
        token = LANES // 4 - token_shift[where, :]
        hit = ((token >> 1) == iota((LANES, LANES), 1)).astype(F32).astype(BF16)
        left_terms[where, 0:LANES] = hit
        left_terms[where, LANES:] = jnp.maximum(act_ref[where, :], 0.0).astype(BF16)
    padded = -(-3 * pairs // 16) * 16
    for c in range(channels):
        at = slice(c % 2 * LANES, (c % 2 + 1) * LANES)
        rows = [
            table_rows[pl.ds(8 * channels * g + c, 8, stride=channels), :]
            for g in range(3 * pairs // 8)
        ]
        rows.append(jnp.zeros((padded - 3 * pairs, LANES), F32))
        right_terms[c // 2, 0:padded, at] = jnp.concatenate(rows, axis=0).astype(BF16)
        right_terms[c // 2, padded:LANES, at] = jnp.zeros((LANES - padded, LANES), BF16)
        right_terms[c // 2, LANES:, at] = jnp.broadcast_to(
            w_query[:, c : c + 1], (width, LANES)
        ).astype(BF16)

    def band_step(step, carry):
        for c in range(2):
            band = dot(left_terms[first_query:query_end, :], right_terms[2 * step + c])
            for d in range(2):
                at = slice(d * LANES, (d + 1) * LANES)
                band_ref[4 * step + 2 * c + d, first_query:query_end, :] = band[:, at]
        return carry

    lax.fori_loop(0, channels // 4, band_step, 0)

    copy.wait()
    lane = iota((channels, LANES), 1)
    lane8 = iota((8, LANES), 1)
    log2e = math.log2(math.e)

    def key_start(n):
        return HALO + QB * n + scalars[0, n + offset_lanes - 2 * HALO // QB]

    def column_stage(step, w):
        n = (step * PAIR_GROUP + w)
        query = pl.multiple_of(first_query + QB * n, QB)
        start = key_start(n)
        tile = start // LANES
        shift = start % LANES
        back = LANES - shift
        key_tokens = pltpu.roll(
            jnp.where(lane8 >= shift, token_rows[tile], token_rows[tile + 1]), back, 1
        )
        side_ref[w] = pltpu.roll(
            jnp.where(lane >= shift, key_terms[tile], key_terms[tile + 1]), back, 1
        )
        for g in range(QB // 8):
            rows = pl.ds(query + 8 * g, 8)
            column_ref[w, 8 * g : 8 * g + 8, :] = (
                jnp.clip(key_tokens + token_shift[rows, :], 0, LANES // 2 - 1)
                + token_base[rows, :]
            )

    def start_stage(step, w):
        query = pl.multiple_of(first_query + QB * (step * PAIR_GROUP + w), QB)
        slot = step % PAIR_SLOTS
        for g in range(QB // 8):
            half, part = g // (group // 8), g % (group // 8)
            at = slice(half * LANES, (half + 1) * LANES)
            column = column_ref[w, 8 * g : 8 * g + 8, :]
            rows = pl.ds(query + 8 * g, 8)
            for e in range(channels):
                row = e * group + 8 * part
                start_ref[slot, w, row : row + 8, at] = jnp.take_along_axis(
                    band_ref[e, rows, :], column, axis=1, mode="promise_in_bounds"
                ) + jnp.broadcast_to(side_ref[w, e : e + 1, :], (8, LANES))

    def relu(values):
        return jnp.maximum(values.astype(BF16), jnp.zeros((), BF16))

    def first_stage(step, w):
        slot = (step + 3) % PAIR_SLOTS
        second_ref[w] = relu(dot(mlp_ref[0], relu(start_ref[slot, w])))

    def second_stage(w):
        third_ref[w] = relu(dot(mlp_ref[1], second_ref[w]))

    def norm_stage(step, w):
        slot = (step + 1) % PAIR_SLOTS
        third = dot(mlp_ref[2], third_ref[w])
        for half in range(2):
            at = slice(half * LANES, (half + 1) * LANES)
            normed = []
            for part in range(group // 8):
                pair = [
                    third[e * group + 8 * part : e * group + 8 * part + 8, at]
                    + start_ref[slot, w, e * group + 8 * part : e * group + 8 * part + 8, at]
                    for e in range(channels)
                ]
                centre = sum(pair[1:], pair[0]) * (1.0 / channels)
                shifted = [p - centre for p in pair]
                spread = sum([s * s for s in shifted[1:]], shifted[0] * shifted[0])
                factor = lax.rsqrt(spread * (1.0 / channels) + EPSILON) * log2e
                normed.append([s * factor for s in shifted])
            for e in range(channels):
                rows = jnp.concatenate([n[e] for n in normed], axis=0)
                normed_ref[w, e * group : (e + 1) * group, at] = rows.astype(BF16)

    def bias_stage(step, w):
        n = (step - PAIR_DEPTH) * PAIR_GROUP + w
        bias = dot(bias_weight_ref[...], normed_ref[w])
        for layer in range(BLOCKS):
            part = bias[layer * per_block : (layer + 1) * per_block]
            bias_ref[n, layer, 0:per_block, :] = part[:, 0:LANES]
            bias_ref[n, layer, per_block : 2 * per_block, :] = part[:, LANES:]

    groups = window_count // PAIR_GROUP

    def pair_step(step, carry=None):
        def live(behind):
            return not isinstance(step, int) or 0 <= step - behind < groups

        for w in range(PAIR_GROUP):
            if live(4):
                bias_stage(step, w)
            if live(3):
                norm_stage(step, w)
            if live(2):
                second_stage(w)
            if live(1):
                first_stage(step, w)
            if live(0):
                column_stage(step, w)
                start_stage(step, w)
        return carry

    for step in range(PAIR_DEPTH):
        pair_step(step)
    lax.fori_loop(PAIR_DEPTH, groups, pair_step, 0)
    for step in range(groups, groups + PAIR_DEPTH):
        pair_step(step)

    for copy in weight_copies[3:]:
        copy.wait()
    head_of_lane = iota((QB // 2, width), 1) // head_size
    scale = log2e / math.sqrt(head_size)

    def project(layer, first, rows, chunk):
        w_first = jnp.concatenate([w_attn_ref[layer, 0], w_attn_ref[layer, 1]], axis=1)
        w_second = jnp.concatenate([w_attn_ref[layer, 2], w_attn_ref[layer, 3]], axis=1)
        for row in range(first, first + rows, chunk):
            where = slice(row, row + chunk)
            normed = normalize(act_ref[where, :], 1).astype(BF16)
            held = held_ref[where, :] > 0.0
            both = dot(normed, w_first)
            query_ref[where, :] = (both[:, :width] * scale).astype(BF16)
            key_ref[where, :] = jnp.where(held, both[:, width:], 0.0)
            both = dot(normed, w_second)
            value_ref[where, :] = jnp.where(held, both[:, :width], 0.0)
            gate_ref[where, :] = jax.nn.sigmoid(both[:, width:])

    def attend(layer, n):
        query = pl.multiple_of(first_query + QB * n, QB)
        start = key_start(n)
        q = query_ref[pl.ds(query, QB), :]
        k = key_ref[pl.ds(start, KW), :].astype(BF16)
        v = jnp.concatenate(
            [value_ref[pl.ds(start, KW), :], held_ref[pl.ds(start, KW), :]], axis=1
        ).astype(BF16)
        blocks = []
        for half in range(2):
            part = q[half * QB // 2 : (half + 1) * QB // 2]
            for h in range(heads):
                blocks.append(jnp.where(head_of_lane == h, part, jnp.zeros((), BF16)))
        scores = dot_nt(jnp.concatenate(blocks, axis=0), k) + bias_ref[n, layer]
        sums = dot(jnp.exp2(scores).astype(BF16), v)
        halves = []
        for half in range(2):
            base = half * per_block
            value = sums[base : base + group, :LANES]
            total = sums[base : base + group, LANES:]
            for h in range(1, heads):
                row = base + h * group
                value = jnp.where(head_of_lane == h, sums[row : row + group, :LANES], value)
                total = jnp.where(head_of_lane == h, sums[row : row + group, LANES:], total)
            halves.append(value / total)
        attended = jnp.concatenate(halves, axis=0)
        gated_ref[pl.ds(query, QB), :] = (attended * gate_ref[pl.ds(query, QB), :]).astype(BF16)

    def dense(layer, first, rows, chunk):
        for row in range(first, first + rows, chunk):
            where = slice(row, row + chunk)
            act = act_ref[where, :] + dot(gated_ref[where, :], w_out_ref[layer])
            act = jnp.where(held_ref[where, :] > 0.0, act, 0.0)
            normed = normalize(act, 1).astype(BF16)
            gate_part = dot(normed, w_in_ref[layer, 0])
            up_part = dot(normed, w_in_ref[layer, 1])
            hidden = (gate_part / (1.0 + jnp.exp(-gate_part)) * up_part).astype(BF16)
            act_ref[where, :] = act + dot(hidden, w_trans_out_ref[layer])

    chunk_of = (288, 336, 240)
    for layer in range(BLOCKS):
        first_window = layer * HALO // QB
        last_window = window_count - layer * HALO // QB
        windows = last_window - first_window
        query_first = first_query + QB * first_window
        query_rows = QB * windows
        key_first = query_first - HALO
        key_rows = query_rows + 2 * HALO
        project(layer, key_first, key_rows, key_rows // 3)

        def attend_step(step, carry):
            for w in range(windows // 3):
                attend(layer, first_window + step * (windows // 3) + w)
            return carry

        lax.fori_loop(0, 3, attend_step, 0)
        dense(layer, query_first, query_rows, chunk_of[layer])

    atom_out_ref[...] = act_ref[atoms : 2 * atoms, :].astype(BF16)
    reach = atoms + LANES
    feature_ref[atoms + HALO : reach, :] = jnp.zeros_like(feature_ref[atoms + HALO : reach, :])
    for row in range(0, atoms + HALO, 160):
        rows = act_ref[atoms + row : atoms + row + 160, :].astype(BF16)
        features = jnp.maximum(dot(rows, w_token_ref[...]), 0.0)
        feature_ref[row : row + 160, :] = features.astype(BF16)
    slot = iota((tokens, LANES), 0) + tokens
    member = jnp.concatenate(
        [
            (slot == relative_int[tile : tile + 1]).astype(F32)
            for tile in range(tiles, 2 * tiles + 1)
        ],
        axis=1,
    ).astype(BF16)
    sums = dot(member, feature_ref[...])
    diagonal = (iota((tokens, LANES), 0) == iota((tokens, LANES), 1)).astype(F32)
    atoms_of = jnp.sum(diagonal * metas[1][4:5], axis=1, keepdims=True)
    token_out_ref[...] = (sums / atoms_of).astype(BF16)


def shards(
    atom_single,
    atom_token,
    token_atoms,
    window_offset,
    token_pair,
    w_zpair,
    w_single,
    w_pair_mlp,
    w_bias,
    w_attn,
    w_out,
    w_trans_in,
    w_trans_out,
    w_token,
):
    index, count = shard_place()
    atoms, width = atom_single.shape
    tokens, band, depth = token_pair.shape
    channels = w_zpair.shape[1]
    tiles = atoms // LANES
    pairs = tokens * band // LANES
    payload_rows = atoms + channels * pairs + 16

    vmem = pl.BlockSpec(memory_space=pltpu.VMEM)
    anywhere = pl.BlockSpec(memory_space=pl.ANY)
    parts = 3
    payload = pl.pallas_call(
        project_kernel,
        out_shape=jax.ShapeDtypeStruct((payload_rows, width), BF16),
        in_specs=[anywhere] * 6,
        out_specs=anywhere,
        scratch_shapes=[
            pltpu.VMEM((tokens * band, depth), BF16),
            pltpu.VMEM((channels, depth), BF16),
            pltpu.VMEM((atoms,), jnp.int32),
            pltpu.VMEM((tokens,), jnp.int32),
            pltpu.VMEM(window_offset.shape, jnp.int32),
            pltpu.VMEM((payload_rows - atoms, width), BF16),
            pltpu.VMEM((16, width), F32),
            pltpu.SemaphoreType.DMA((4,)),
            pltpu.SemaphoreType.DMA((parts,)),
            pltpu.SemaphoreType.DMA((parts + 1,)),
        ],
        name="project",
    )(
        token_pair.reshape(tokens * band, depth),
        jnp.swapaxes(w_zpair, 0, 1),
        atom_single,
        atom_token,
        token_atoms,
        window_offset,
    )
    near = [(i, i ^ 1) for i in range(count)]
    far = [(i, ((i + 1) ^ 1) - 1) for i in range(1, count - 1)]
    first_side = lax.ppermute(payload, RING, near)
    second_side = lax.ppermute(payload, RING, far)

    weights = (
        jnp.swapaxes(w_single, 1, 2),
        w_pair_mlp,
        jnp.swapaxes(w_bias, 1, 2),
        w_attn,
        w_out,
        w_trans_in,
        w_trans_out,
        w_token,
    )
    in_hbm = pl.BlockSpec(memory_space=pltpu.HBM)
    reach = 3 * atoms
    windows = (atoms + 5 * HALO) // QB
    heads = w_bias.shape[2]
    channels_out = w_token.shape[1]
    token_single, atom_out = pl.pallas_call(
        main_kernel,
        out_shape=(
            jax.ShapeDtypeStruct((tokens, channels_out), BF16),
            jax.ShapeDtypeStruct((atoms, width), BF16),
        ),
        in_specs=[in_hbm] + [anywhere] * 2 + [in_hbm] * len(weights),
        out_specs=(vmem, vmem),
        scratch_shapes=[
            pltpu.VMEM((3, payload_rows, width), BF16),
            *[pltpu.VMEM(w.shape, BF16) for w in weights],
            pltpu.VMEM((8, LANES), jnp.int32),
            pltpu.SMEM((8, LANES), jnp.int32),
            pltpu.VMEM((3 * tiles + 1, 8, LANES), jnp.int32),
            pltpu.VMEM((3 * tiles + 1, channels, LANES), F32),
            pltpu.VMEM((reach, LANES), jnp.int32),
            pltpu.VMEM((reach, LANES), jnp.int32),
            pltpu.VMEM((3 * pairs * channels, LANES), F32),
            pltpu.VMEM((channels, reach, LANES), F32),
            pltpu.VMEM((PAIR_GROUP, channels, LANES), F32),
            pltpu.VMEM((PAIR_GROUP, QB, LANES), jnp.int32),
            pltpu.VMEM((PAIR_SLOTS, PAIR_GROUP, 256, 256), F32),
            *[pltpu.VMEM((PAIR_GROUP, 256, 256), BF16)] * 3,
            pltpu.VMEM((reach, 256), BF16),
            pltpu.VMEM((channels // 2, 256, 256), BF16),
            pltpu.VMEM((3, 256, 256), BF16),
            pltpu.VMEM((BLOCKS * heads * 256 // channels, 256), BF16),
            pltpu.VMEM((windows, BLOCKS, heads * QB, KW), F32),
            pltpu.VMEM((reach, width), F32),
            pltpu.VMEM((reach, LANES), F32),
            pltpu.VMEM((reach, width), BF16),
            pltpu.VMEM((reach, width), F32),
            pltpu.VMEM((reach, width), F32),
            pltpu.VMEM((reach, width), F32),
            pltpu.VMEM((reach, width), BF16),
            pltpu.VMEM((atoms + LANES, channels_out), BF16),
            pltpu.SemaphoreType.DMA((4,)),
            pltpu.SemaphoreType.DMA((len(weights),)),
        ],
        compiler_params=pltpu.CompilerParams(vmem_limit_bytes=48 * 2**20),
        name="encode",
    )(
        pltpu.with_memory_space_constraint(payload, pltpu.HBM),
        first_side,
        second_side,
        *[pltpu.with_memory_space_constraint(w, pltpu.HBM) for w in weights],
    )
    return token_single, atom_out


def solution(mesh):
    split = ("group", "seq", "chan", "sub")
    in_specs = (
        P(split, None),
        P(split),
        P(split),
        P(split),
        P(split, None, None),
        P(),
        P(),
        P(),
        P(),
        P(),
        P(),
        P(),
        P(),
        P(),
    )
    out_specs = (P(split, None), P(split, None))
    return jax.shard_map(shards, mesh=mesh, in_specs=in_specs, out_specs=out_specs, check_vma=False)
```

```python
import math

import jax
import jax.numpy as jnp
from jax import lax
from jax.experimental import pallas as pl
from jax.experimental.pallas import tpu as pltpu
from jax.sharding import PartitionSpec as P

BLOCKS = 3
QB = 32
KW = 128
HALO = 96
LANES = 128
PAIR_DEPTH = 4
PAIR_SLOTS = 4
PAIR_GROUP = 3
EPSILON = 1e-05
RING = ("seq", "chan", "sub")
NT = (((1,), (1,)), ((), ()))
F32 = jnp.float32
BF16 = jnp.bfloat16


def dot(a, b):
    return jnp.dot(a, b, preferred_element_type=F32)


def dot_nt(a, b):
    return lax.dot_general(a, b, NT, preferred_element_type=F32)


def iota(shape, axis):
    return lax.broadcasted_iota(jnp.int32, shape, axis)


def shard_place():
    index, count = 0, 1
    for name in RING:
        index = index * lax.axis_size(name) + lax.axis_index(name)
        count = count * lax.axis_size(name)
    return index, count


def normalize(values, axis):
    centre = jnp.mean(values, axis=axis, keepdims=True)
    shifted = values - centre
    spread = jnp.mean(shifted * shifted, axis=axis, keepdims=True)
    return shifted * lax.rsqrt(spread + EPSILON)


def project_kernel(
    pair_hbm,
    wz_hbm,
    atom_hbm,
    token_hbm,
    atoms_of_hbm,
    offset_hbm,
    out_hbm,
    pair_ref,
    wz_ref,
    token_ref,
    atoms_of_ref,
    offset_ref,
    band_ref,
    meta_ref,
    small_sems,
    in_sems,
    out_sems,
):
    rows, width = pair_ref.shape
    atoms = atom_hbm.shape[0]
    tokens = atoms_of_hbm.shape[0]
    channels = wz_hbm.shape[0]
    tiles = atoms // LANES
    parts = in_sems.shape[0]
    step = rows // parts
    band_step = channels * step // LANES
    meta = atoms + channels * rows // LANES

    loads = [
        pltpu.make_async_copy(
            pair_hbm.at[pl.ds(step * part, step)],
            pair_ref.at[pl.ds(step * part, step)],
            in_sems.at[part],
        )
        for part in range(parts)
    ]
    small = [
        pltpu.make_async_copy(wz_hbm, wz_ref, small_sems.at[0]),
        pltpu.make_async_copy(token_hbm, token_ref, small_sems.at[1]),
        pltpu.make_async_copy(atoms_of_hbm, atoms_of_ref, small_sems.at[2]),
        pltpu.make_async_copy(offset_hbm, offset_ref, small_sems.at[3]),
    ]
    atom_copy = pltpu.make_async_copy(atom_hbm, out_hbm.at[pl.ds(0, atoms)], out_sems.at[parts])
    loads[0].start()
    for copy in small + loads[1:]:
        copy.start()
    atom_copy.start()

    eye = iota((width, width), 0) == iota((width, width), 1)
    centring = (eye.astype(F32) - 1.0 / width).astype(BF16)
    average = jnp.full((channels, width), 1.0 / width, BF16)
    for copy in small:
        copy.wait()
    index, _ = shard_place()
    meta_ref[...] = jnp.zeros_like(meta_ref)
    base = (index - 1) * tokens
    for tile in range(tiles):
        local = token_ref[LANES * tile : LANES * (tile + 1)].reshape(1, LANES) - base
        meta_ref[tile : tile + 1, :] = local.astype(F32)
    meta_ref[tiles : tiles + 1, 0 : offset_ref.shape[0]] = (
        offset_ref[...].reshape(1, offset_ref.shape[0]).astype(F32)
    )
    meta_ref[tiles + 1 : tiles + 2, 0:tokens] = (
        atoms_of_ref[...].reshape(1, tokens).astype(F32)
    )
    band_ref[meta - atoms :, :] = meta_ref[...].astype(BF16)
    stores = []
    for part in range(parts):
        loads[part].wait()
        shifted = dot(pair_ref[step * part : step * (part + 1), :], centring)
        spread = dot_nt(average, (shifted * shifted).astype(BF16))
        projected = dot_nt(wz_ref[...], shifted.astype(BF16))
        projected = (projected * lax.rsqrt(spread + EPSILON)).astype(BF16)
        for tile in range(step // LANES):
            row = band_step * part + channels * tile
            band_ref[row : row + channels, :] = projected[:, LANES * tile : LANES * (tile + 1)]
        first, count = band_step * part, band_step + (16 if part == parts - 1 else 0)
        copy = pltpu.make_async_copy(
            band_ref.at[pl.ds(first, count)],
            out_hbm.at[pl.ds(atoms + first, count)],
            out_sems.at[part],
        )
        copy.start()
        stores.append(copy)
    for copy in stores:
        copy.wait()
    atom_copy.wait()


def main_kernel(
    own_hbm,
    near_hbm,
    far_hbm,
    w_single_hbm,
    w_mlp_hbm,
    w_bias_hbm,
    w_attn_hbm,
    w_out_hbm,
    w_in_hbm,
    w_trans_out_hbm,
    w_token_hbm,
    token_out_ref,
    atom_out_ref,
    payload_ref,
    w_single_ref,
    w_mlp_ref,
    w_bias_ref,
    w_attn_ref,
    w_out_ref,
    w_in_ref,
    w_trans_out_ref,
    w_token_ref,
    scalars_vmem,
    scalars,
    token_rows,
    key_terms,
    token_shift,
    token_base,
    table_rows,
    band_ref,
    side_ref,
    column_ref,
    start_ref,
    second_ref,
    third_ref,
    normed_ref,
    left_terms,
    right_terms,
    mlp_ref,
    bias_weight_ref,
    bias_ref,
    act_ref,
    held_ref,
    query_ref,
    gate_ref,
    key_ref,
    value_ref,
    gated_ref,
    feature_ref,
    sems,
    weight_sems,
):
    index, count = shard_place()
    atoms, width = atom_out_ref.shape
    tokens = token_out_ref.shape[0]
    channels = w_mlp_ref.shape[1]
    heads = w_bias_ref.shape[1]
    head_size = width // heads
    tiles = atoms // LANES
    pairs = tokens // 2
    meta = atoms + channels * pairs
    first_valid = jnp.where(index == 0, atoms, 0)
    end_valid = jnp.where(index == count - 1, 2 * atoms, 3 * atoms)
    first_query = 2 * HALO
    window_count = (atoms + HALO + 4 * HALO) // QB
    query_end = first_query + QB * window_count

    even = index % 2 == 0
    copies = [
        pltpu.make_async_copy(own_hbm, payload_ref.at[1], sems.at[0]),
        pltpu.make_async_copy(near_hbm, payload_ref.at[jnp.where(even, 2, 0)], sems.at[1]),
        pltpu.make_async_copy(far_hbm, payload_ref.at[jnp.where(even, 0, 2)], sems.at[2]),
    ]
    weight_copies = [
        pltpu.make_async_copy(source, target, weight_sems.at[i])
        for i, (source, target) in enumerate(
            (
                (w_mlp_hbm, w_mlp_ref),
                (w_bias_hbm, w_bias_ref),
                (w_single_hbm, w_single_ref),
                (w_attn_hbm, w_attn_ref),
                (w_out_hbm, w_out_ref),
                (w_in_hbm, w_in_ref),
                (w_trans_out_hbm, w_trans_out_ref),
                (w_token_hbm, w_token_ref),
            )
        )
    ]
    for copy in weight_copies[:3] + copies + weight_copies[3:]:
        copy.start()
    for copy in weight_copies[:3]:
        copy.wait()

    big = 256
    group = big // channels
    select = (iota((big, channels), 0) // group == iota((big, channels), 1)).astype(BF16)
    same_query = (iota((big, big), 0) % group) == (iota((big, big), 1) % group)
    for layer in range(3):
        by_row = dot_nt(select, w_mlp_ref[layer]).astype(BF16)
        mlp_ref[layer] = jnp.where(same_query, dot_nt(by_row, select), 0.0).astype(BF16)
    per_block = heads * group
    pick_head = (iota((per_block, heads), 0) // group == iota((per_block, heads), 1)).astype(BF16)
    for layer in range(BLOCKS):
        by_row = dot(pick_head, w_bias_ref[layer]).astype(BF16)
        bias_weight_ref[layer * per_block : (layer + 1) * per_block, :] = jnp.where(
            same_query[0:per_block], dot_nt(by_row, select), 0.0
        ).astype(BF16)

    for copy in copies:
        copy.wait()
    sides = tuple(payload_ref.at[side] for side in range(3))
    metas = [ref[meta : meta + 16, :].astype(F32) for ref in sides]
    number = iota((3 * tiles, LANES), 0) * LANES + iota((3 * tiles, LANES), 1)
    relative = jnp.concatenate(
        [m[0:tiles] + s for m, s in zip(metas, (-tokens, 0, tokens))], axis=0
    )
    inside = (number >= first_valid) & (number < end_valid)
    relative = jnp.where(inside, relative, -64.0)
    relative_int = relative.astype(jnp.int32)
    offset_lanes = atoms // QB
    offset_row = (
        metas[0][3:4]
        + pltpu.roll(metas[1][3:4], offset_lanes, 1)
        + pltpu.roll(metas[2][3:4], 2 * offset_lanes, 1)
    )
    scalars_vmem[...] = jnp.broadcast_to(offset_row, (8, LANES)).astype(jnp.int32)
    copy = pltpu.make_async_copy(scalars_vmem, scalars, sems.at[3])
    copy.start()
    for tile in range(3 * tiles):
        token_rows[tile] = jnp.broadcast_to(relative_int[tile : tile + 1], (8, LANES))
    token_rows[3 * tiles] = jnp.zeros((8, LANES), jnp.int32)

    eye = iota((LANES, LANES), 0) == iota((LANES, LANES), 1)
    ones = jnp.ones((LANES, LANES), BF16)
    for side, ref in enumerate(sides):
        for tile in range(tiles):
            rows = ref[tile * LANES : (tile + 1) * LANES, :]
            at = side * tiles + tile
            where = slice(at * LANES, (at + 1) * LANES)
            act_ref[where, :] = rows.astype(F32)
            held_ref[where, :] = (
                (iota((LANES, LANES), 0) + at * LANES >= first_valid)
                & (iota((LANES, LANES), 0) + at * LANES < end_valid)
            ).astype(F32)
            relu = jnp.maximum(rows, jnp.zeros((), BF16))
            key_terms[at] = dot_nt(w_single_ref[1], relu).astype(BF16).astype(F32)
            column = dot(jnp.where(eye, relative[at : at + 1], 0.0).astype(BF16), ones)
            column = column.astype(jnp.int32)
            base = (column & 1) * (LANES // 2)
            token_base[where, :] = base
            token_shift[where, :] = LANES // 4 - column
        for pair in range(pairs):
            row = atoms + channels * pair
            to = (side * pairs + pair) * channels
            table_rows[to : to + channels, :] = ref[row : row + channels, :].astype(F32)
    key_terms[3 * tiles] = jnp.zeros((channels, LANES), F32)

    w_query = jnp.transpose(w_single_ref[0].astype(F32))
    for tile in range(first_query // LANES, -(-query_end // LANES)):
        where = slice(tile * LANES, (tile + 1) * LANES)
        token = LANES // 4 - token_shift[where, :]
        hit = ((token >> 1) == iota((LANES, LANES), 1)).astype(F32).astype(BF16)
        left_terms[where, 0:LANES] = hit
        left_terms[where, LANES:] = jnp.maximum(act_ref[where, :], 0.0).astype(BF16)
    padded = -(-3 * pairs // 16) * 16
    for c in range(channels):
        at = slice(c % 2 * LANES, (c % 2 + 1) * LANES)
        rows = [
            table_rows[pl.ds(8 * channels * g + c, 8, stride=channels), :]
            for g in range(3 * pairs // 8)
        ]
        rows.append(jnp.zeros((padded - 3 * pairs, LANES), F32))
        right_terms[c // 2, 0:padded, at] = jnp.concatenate(rows, axis=0).astype(BF16)
        right_terms[c // 2, padded:LANES, at] = jnp.zeros((LANES - padded, LANES), BF16)
        right_terms[c // 2, LANES:, at] = jnp.broadcast_to(
            w_query[:, c : c + 1], (width, LANES)
        ).astype(BF16)

    def band_step(step, carry):
        for c in range(2):
            band = dot(left_terms[first_query:query_end, :], right_terms[2 * step + c])
            for d in range(2):
                at = slice(d * LANES, (d + 1) * LANES)
                band_ref[4 * step + 2 * c + d, first_query:query_end, :] = band[:, at]
        return carry

    lax.fori_loop(0, channels // 4, band_step, 0)

    copy.wait()
    lane = iota((channels, LANES), 1)
    lane8 = iota((8, LANES), 1)
    log2e = math.log2(math.e)

    def key_start(n):
        return HALO + QB * n + scalars[0, n + offset_lanes - 2 * HALO // QB]

    def column_stage(step, w):
        n = (step * PAIR_GROUP + w)
        query = pl.multiple_of(first_query + QB * n, QB)
        start = key_start(n)
        tile = start // LANES
        shift = start % LANES
        back = LANES - shift
        key_tokens = pltpu.roll(
            jnp.where(lane8 >= shift, token_rows[tile], token_rows[tile + 1]), back, 1
        )
        side_ref[w] = pltpu.roll(
            jnp.where(lane >= shift, key_terms[tile], key_terms[tile + 1]), back, 1
        )
        for g in range(QB // 8):
            rows = pl.ds(query + 8 * g, 8)
            column_ref[w, 8 * g : 8 * g + 8, :] = (
                jnp.clip(key_tokens + token_shift[rows, :], 0, LANES // 2 - 1)
                + token_base[rows, :]
            )

    def start_stage(step, w):
        query = pl.multiple_of(first_query + QB * (step * PAIR_GROUP + w), QB)
        slot = step % PAIR_SLOTS
        for g in range(QB // 8):
            half, part = g // (group // 8), g % (group // 8)
            at = slice(half * LANES, (half + 1) * LANES)
            column = column_ref[w, 8 * g : 8 * g + 8, :]
            rows = pl.ds(query + 8 * g, 8)
            for e in range(channels):
                row = e * group + 8 * part
                start_ref[slot, w, row : row + 8, at] = jnp.take_along_axis(
                    band_ref[e, rows, :], column, axis=1, mode="promise_in_bounds"
                ) + jnp.broadcast_to(side_ref[w, e : e + 1, :], (8, LANES))

    def relu(values):
        return jnp.maximum(values.astype(BF16), jnp.zeros((), BF16))

    def first_stage(step, w):
        slot = (step + 3) % PAIR_SLOTS
        second_ref[w] = relu(dot(mlp_ref[0], relu(start_ref[slot, w])))

    def second_stage(w):
        third_ref[w] = relu(dot(mlp_ref[1], second_ref[w]))

    def norm_stage(step, w):
        slot = (step + 1) % PAIR_SLOTS
        third = dot(mlp_ref[2], third_ref[w])
        for half in range(2):
            at = slice(half * LANES, (half + 1) * LANES)
            normed = []
            for part in range(group // 8):
                pair = [
                    third[e * group + 8 * part : e * group + 8 * part + 8, at]
                    + start_ref[slot, w, e * group + 8 * part : e * group + 8 * part + 8, at]
                    for e in range(channels)
                ]
                centre = sum(pair[1:], pair[0]) * (1.0 / channels)
                shifted = [p - centre for p in pair]
                spread = sum([s * s for s in shifted[1:]], shifted[0] * shifted[0])
                factor = lax.rsqrt(spread * (1.0 / channels) + EPSILON) * log2e
                normed.append([s * factor for s in shifted])
            for e in range(channels):
                rows = jnp.concatenate([n[e] for n in normed], axis=0)
                normed_ref[w, e * group : (e + 1) * group, at] = rows.astype(BF16)

    def bias_stage(step, w):
        n = (step - PAIR_DEPTH) * PAIR_GROUP + w
        bias = dot(bias_weight_ref[...], normed_ref[w])
        for layer in range(BLOCKS):
            part = bias[layer * per_block : (layer + 1) * per_block]
            bias_ref[n, layer, 0:per_block, :] = part[:, 0:LANES]
            bias_ref[n, layer, per_block : 2 * per_block, :] = part[:, LANES:]

    groups = window_count // PAIR_GROUP

    def pair_step(step, carry=None):
        def live(behind):
            return not isinstance(step, int) or 0 <= step - behind < groups

        for w in range(PAIR_GROUP):
            if live(4):
                bias_stage(step, w)
            if live(3):
                norm_stage(step, w)
            if live(2):
                second_stage(w)
            if live(1):
                first_stage(step, w)
            if live(0):
                column_stage(step, w)
                start_stage(step, w)
        return carry

    for step in range(PAIR_DEPTH):
        pair_step(step)
    lax.fori_loop(PAIR_DEPTH, groups, pair_step, 0)
    for step in range(groups, groups + PAIR_DEPTH):
        pair_step(step)

    for copy in weight_copies[3:]:
        copy.wait()
    head_of_lane = iota((QB // 2, width), 1) // head_size
    scale = log2e / math.sqrt(head_size)

    def project(layer, first, rows, chunk):
        w_first = jnp.concatenate([w_attn_ref[layer, 0], w_attn_ref[layer, 1]], axis=1)
        w_second = jnp.concatenate([w_attn_ref[layer, 2], w_attn_ref[layer, 3]], axis=1)
        for row in range(first, first + rows, chunk):
            where = slice(row, row + chunk)
            normed = normalize(act_ref[where, :], 1).astype(BF16)
            held = held_ref[where, :] > 0.0
            both = dot(normed, w_first)
            query_ref[where, :] = (both[:, :width] * scale).astype(BF16)
            key_ref[where, :] = jnp.where(held, both[:, width:], 0.0)
            both = dot(normed, w_second)
            value_ref[where, :] = jnp.where(held, both[:, :width], 0.0)
            gate_ref[where, :] = jax.nn.sigmoid(both[:, width:])

    def attend(layer, n):
        query = pl.multiple_of(first_query + QB * n, QB)
        start = key_start(n)
        q = query_ref[pl.ds(query, QB), :]
        k = key_ref[pl.ds(start, KW), :].astype(BF16)
        v = jnp.concatenate(
            [value_ref[pl.ds(start, KW), :], held_ref[pl.ds(start, KW), :]], axis=1
        ).astype(BF16)
        blocks = []
        for half in range(2):
            part = q[half * QB // 2 : (half + 1) * QB // 2]
            for h in range(heads):
                blocks.append(jnp.where(head_of_lane == h, part, jnp.zeros((), BF16)))
        scores = dot_nt(jnp.concatenate(blocks, axis=0), k) + bias_ref[n, layer]
        sums = dot(jnp.exp2(scores).astype(BF16), v)
        halves = []
        for half in range(2):
            base = half * per_block
            value = sums[base : base + group, :LANES]
            total = sums[base : base + group, LANES:]
            for h in range(1, heads):
                row = base + h * group
                value = jnp.where(head_of_lane == h, sums[row : row + group, :LANES], value)
                total = jnp.where(head_of_lane == h, sums[row : row + group, LANES:], total)
            halves.append(value / total)
        attended = jnp.concatenate(halves, axis=0)
        gated_ref[pl.ds(query, QB), :] = (attended * gate_ref[pl.ds(query, QB), :]).astype(BF16)

    def dense(layer, first, rows, chunk):
        for row in range(first, first + rows, chunk):
            where = slice(row, row + chunk)
            act = act_ref[where, :] + dot(gated_ref[where, :], w_out_ref[layer])
            act = jnp.where(held_ref[where, :] > 0.0, act, 0.0)
            normed = normalize(act, 1).astype(BF16)
            gate_part = dot(normed, w_in_ref[layer, 0])
            up_part = dot(normed, w_in_ref[layer, 1])
            hidden = (gate_part / (1.0 + jnp.exp(-gate_part)) * up_part).astype(BF16)
            act_ref[where, :] = act + dot(hidden, w_trans_out_ref[layer])

    chunk_of = (864, 672, 480)
    for layer in range(BLOCKS):
        first_window = layer * HALO // QB
        last_window = window_count - layer * HALO // QB
        windows = last_window - first_window
        query_first = first_query + QB * first_window
        query_rows = QB * windows
        key_first = query_first - HALO
        key_rows = query_rows + 2 * HALO
        project(layer, key_first, key_rows, key_rows // 3)

        def attend_step(step, carry):
            for w in range(windows // 3):
                attend(layer, first_window + step * (windows // 3) + w)
            return carry

        for step in range(3):
            attend_step(step, 0)
        dense(layer, query_first, query_rows, chunk_of[layer])

    atom_out_ref[...] = act_ref[atoms : 2 * atoms, :].astype(BF16)
    reach = atoms + LANES
    feature_ref[atoms + HALO : reach, :] = jnp.zeros_like(feature_ref[atoms + HALO : reach, :])
    for row in range(0, atoms + HALO, 160):
        rows = act_ref[atoms + row : atoms + row + 160, :].astype(BF16)
        features = jnp.maximum(dot(rows, w_token_ref[...]), 0.0)
        feature_ref[row : row + 160, :] = features.astype(BF16)
    slot = iota((tokens, LANES), 0) + tokens
    member = jnp.concatenate(
        [
            (slot == relative_int[tile : tile + 1]).astype(F32)
            for tile in range(tiles, 2 * tiles + 1)
        ],
        axis=1,
    ).astype(BF16)
    sums = dot(member, feature_ref[...])
    diagonal = (iota((tokens, LANES), 0) == iota((tokens, LANES), 1)).astype(F32)
    atoms_of = jnp.sum(diagonal * metas[1][4:5], axis=1, keepdims=True)
    token_out_ref[...] = (sums / atoms_of).astype(BF16)


def shards(
    atom_single,
    atom_token,
    token_atoms,
    window_offset,
    token_pair,
    w_zpair,
    w_single,
    w_pair_mlp,
    w_bias,
    w_attn,
    w_out,
    w_trans_in,
    w_trans_out,
    w_token,
):
    index, count = shard_place()
    atoms, width = atom_single.shape
    tokens, band, depth = token_pair.shape
    channels = w_zpair.shape[1]
    tiles = atoms // LANES
    pairs = tokens * band // LANES
    payload_rows = atoms + channels * pairs + 16

    vmem = pl.BlockSpec(memory_space=pltpu.VMEM)
    anywhere = pl.BlockSpec(memory_space=pl.ANY)
    parts = 3
    payload = pl.pallas_call(
        project_kernel,
        out_shape=jax.ShapeDtypeStruct((payload_rows, width), BF16),
        in_specs=[anywhere] * 6,
        out_specs=anywhere,
        scratch_shapes=[
            pltpu.VMEM((tokens * band, depth), BF16),
            pltpu.VMEM((channels, depth), BF16),
            pltpu.VMEM((atoms,), jnp.int32),
            pltpu.VMEM((tokens,), jnp.int32),
            pltpu.VMEM(window_offset.shape, jnp.int32),
            pltpu.VMEM((payload_rows - atoms, width), BF16),
            pltpu.VMEM((16, width), F32),
            pltpu.SemaphoreType.DMA((4,)),
            pltpu.SemaphoreType.DMA((parts,)),
            pltpu.SemaphoreType.DMA((parts + 1,)),
        ],
        name="project",
    )(
        token_pair.reshape(tokens * band, depth),
        jnp.swapaxes(w_zpair, 0, 1),
        atom_single,
        atom_token,
        token_atoms,
        window_offset,
    )
    near = [(i, i ^ 1) for i in range(count)]
    far = [(i, ((i + 1) ^ 1) - 1) for i in range(1, count - 1)]
    first_side = lax.ppermute(payload, RING, near)
    second_side = lax.ppermute(payload, RING, far)

    weights = (
        jnp.swapaxes(w_single, 1, 2),
        w_pair_mlp,
        jnp.swapaxes(w_bias, 1, 2),
        w_attn,
        w_out,
        w_trans_in,
        w_trans_out,
        w_token,
    )
    in_hbm = pl.BlockSpec(memory_space=pltpu.HBM)
    reach = 3 * atoms
    windows = (atoms + 5 * HALO) // QB
    heads = w_bias.shape[2]
    channels_out = w_token.shape[1]
    token_single, atom_out = pl.pallas_call(
        main_kernel,
        out_shape=(
            jax.ShapeDtypeStruct((tokens, channels_out), BF16),
            jax.ShapeDtypeStruct((atoms, width), BF16),
        ),
        in_specs=[in_hbm] + [anywhere] * 2 + [in_hbm] * len(weights),
        out_specs=(vmem, vmem),
        scratch_shapes=[
            pltpu.VMEM((3, payload_rows, width), BF16),
            *[pltpu.VMEM(w.shape, BF16) for w in weights],
            pltpu.VMEM((8, LANES), jnp.int32),
            pltpu.SMEM((8, LANES), jnp.int32),
            pltpu.VMEM((3 * tiles + 1, 8, LANES), jnp.int32),
            pltpu.VMEM((3 * tiles + 1, channels, LANES), F32),
            pltpu.VMEM((reach, LANES), jnp.int32),
            pltpu.VMEM((reach, LANES), jnp.int32),
            pltpu.VMEM((3 * pairs * channels, LANES), F32),
            pltpu.VMEM((channels, reach, LANES), F32),
            pltpu.VMEM((PAIR_GROUP, channels, LANES), F32),
            pltpu.VMEM((PAIR_GROUP, QB, LANES), jnp.int32),
            pltpu.VMEM((PAIR_SLOTS, PAIR_GROUP, 256, 256), F32),
            *[pltpu.VMEM((PAIR_GROUP, 256, 256), BF16)] * 3,
            pltpu.VMEM((reach, 256), BF16),
            pltpu.VMEM((channels // 2, 256, 256), BF16),
            pltpu.VMEM((3, 256, 256), BF16),
            pltpu.VMEM((BLOCKS * heads * 256 // channels, 256), BF16),
            pltpu.VMEM((windows, BLOCKS, heads * QB, KW), F32),
            pltpu.VMEM((reach, width), F32),
            pltpu.VMEM((reach, LANES), F32),
            pltpu.VMEM((reach, width), BF16),
            pltpu.VMEM((reach, width), F32),
            pltpu.VMEM((reach, width), F32),
            pltpu.VMEM((reach, width), F32),
            pltpu.VMEM((reach, width), BF16),
            pltpu.VMEM((atoms + LANES, channels_out), BF16),
            pltpu.SemaphoreType.DMA((4,)),
            pltpu.SemaphoreType.DMA((len(weights),)),
        ],
        compiler_params=pltpu.CompilerParams(vmem_limit_bytes=48 * 2**20),
        name="encode",
    )(
        pltpu.with_memory_space_constraint(payload, pltpu.HBM),
        first_side,
        second_side,
        *[pltpu.with_memory_space_constraint(w, pltpu.HBM) for w in weights],
    )
    return token_single, atom_out


def solution(mesh):
    split = ("group", "seq", "chan", "sub")
    in_specs = (
        P(split, None),
        P(split),
        P(split),
        P(split),
        P(split, None, None),
        P(),
        P(),
        P(),
        P(),
        P(),
        P(),
        P(),
        P(),
        P(),
    )
    out_specs = (P(split, None), P(split, None))
    return jax.shard_map(shards, mesh=mesh, in_specs=in_specs, out_specs=out_specs, check_vma=False)
```

```python
import math

import jax
import jax.numpy as jnp
from jax import lax
from jax.experimental import pallas as pl
from jax.experimental.pallas import tpu as pltpu
from jax.sharding import PartitionSpec as P

BLOCKS = 3
QB = 32
KW = 128
HALO = 96
LANES = 128
PAIR_DEPTH = 4
PAIR_SLOTS = 4
PAIR_GROUP = 3
GROUP_BITS = 4
EARLY = 15
EPSILON = 1e-05
RING = ("seq", "chan", "sub")
NT = (((1,), (1,)), ((), ()))
F32 = jnp.float32
BF16 = jnp.bfloat16


def dot(a, b):
    return jnp.dot(a, b, preferred_element_type=F32)


def dot_nt(a, b):
    return lax.dot_general(a, b, NT, preferred_element_type=F32)


def iota(shape, axis):
    return lax.broadcasted_iota(jnp.int32, shape, axis)


def shard_place():
    index, count = 0, 1
    for name in RING:
        index = index * lax.axis_size(name) + lax.axis_index(name)
        count = count * lax.axis_size(name)
    return index, count


def normalize(values, axis):
    centre = jnp.mean(values, axis=axis, keepdims=True)
    shifted = values - centre
    spread = jnp.mean(shifted * shifted, axis=axis, keepdims=True)
    return shifted * lax.rsqrt(spread + EPSILON)


def project_kernel(
    pair_hbm,
    wz_hbm,
    atom_hbm,
    token_hbm,
    atoms_of_hbm,
    offset_hbm,
    out_hbm,
    pair_ref,
    wz_ref,
    token_ref,
    atoms_of_ref,
    offset_ref,
    band_ref,
    meta_ref,
    small_sems,
    in_sems,
    out_sems,
):
    rows, width = pair_ref.shape
    atoms = atom_hbm.shape[0]
    tokens = atoms_of_hbm.shape[0]
    channels = wz_hbm.shape[0]
    tiles = atoms // LANES
    parts = in_sems.shape[0]
    step = rows // parts
    band_step = channels * step // LANES
    meta = atoms + channels * rows // LANES

    loads = [
        pltpu.make_async_copy(
            pair_hbm.at[pl.ds(step * part, step)],
            pair_ref.at[pl.ds(step * part, step)],
            in_sems.at[part],
        )
        for part in range(parts)
    ]
    small = [
        pltpu.make_async_copy(wz_hbm, wz_ref, small_sems.at[0]),
        pltpu.make_async_copy(token_hbm, token_ref, small_sems.at[1]),
        pltpu.make_async_copy(atoms_of_hbm, atoms_of_ref, small_sems.at[2]),
        pltpu.make_async_copy(offset_hbm, offset_ref, small_sems.at[3]),
    ]
    atom_copy = pltpu.make_async_copy(atom_hbm, out_hbm.at[pl.ds(0, atoms)], out_sems.at[parts])
    loads[0].start()
    for copy in small + loads[1:]:
        copy.start()
    atom_copy.start()

    eye = iota((width, width), 0) == iota((width, width), 1)
    centring = (eye.astype(F32) - 1.0 / width).astype(BF16)
    average = jnp.full((channels, width), 1.0 / width, BF16)
    for copy in small:
        copy.wait()
    index, _ = shard_place()
    meta_ref[...] = jnp.zeros_like(meta_ref)
    base = (index - 1) * tokens
    for tile in range(tiles):
        local = token_ref[LANES * tile : LANES * (tile + 1)].reshape(1, LANES) - base
        meta_ref[tile : tile + 1, :] = local.astype(F32)
    meta_ref[tiles : tiles + 1, 0 : offset_ref.shape[0]] = (
        offset_ref[...].reshape(1, offset_ref.shape[0]).astype(F32)
    )
    meta_ref[tiles + 1 : tiles + 2, 0:tokens] = (
        atoms_of_ref[...].reshape(1, tokens).astype(F32)
    )
    band_ref[meta - atoms :, :] = meta_ref[...].astype(BF16)
    stores = []
    for part in range(parts):
        loads[part].wait()
        shifted = dot(pair_ref[step * part : step * (part + 1), :], centring)
        spread = dot_nt(average, (shifted * shifted).astype(BF16))
        projected = dot_nt(wz_ref[...], shifted.astype(BF16))
        projected = (projected * lax.rsqrt(spread + EPSILON)).astype(BF16)
        for tile in range(step // LANES):
            row = band_step * part + channels * tile
            band_ref[row : row + channels, :] = projected[:, LANES * tile : LANES * (tile + 1)]
        first, count = band_step * part, band_step + (16 if part == parts - 1 else 0)
        copy = pltpu.make_async_copy(
            band_ref.at[pl.ds(first, count)],
            out_hbm.at[pl.ds(atoms + first, count)],
            out_sems.at[part],
        )
        copy.start()
        stores.append(copy)
    for copy in stores:
        copy.wait()
    atom_copy.wait()


class Refs:
    def __init__(self, names, refs):
        self.__dict__.update(zip(names, refs))


PAIR_NAMES = (
    "payload_ref",
    "w_single_ref",
    "w_mlp_ref",
    "w_bias_ref",
    "scalars_vmem",
    "scalars",
    "token_rows",
    "key_terms",
    "token_shift",
    "token_base",
    "table_rows",
    "band_ref",
    "side_ref",
    "column_ref",
    "start_ref",
    "second_ref",
    "third_ref",
    "normed_ref",
    "left_terms",
    "right_terms",
    "mlp_ref",
    "bias_weight_ref",
    "act_ref",
    "held_ref",
    "sems",
)
MAIN_NAMES = (
    "w_attn_ref",
    "w_out_ref",
    "w_in_ref",
    "w_trans_out_ref",
    "w_token_ref",
    "bias_ref",
    "query_ref",
    "gate_ref",
    "key_ref",
    "value_ref",
    "gated_ref",
    "feature_ref",
    "weight_sems",
)


def key_start(r, n):
    offset_lanes = r.act_ref.shape[0] // 3 // QB
    return HALO + QB * n + r.scalars[0, n + offset_lanes - 2 * HALO // QB]


def pair_windows(r, own_hbm, near_hbm, far_hbm, small_hbm, first_window, groups, bias_at):
    index, count = shard_place()
    channels = r.w_mlp_ref.shape[1]
    heads = r.w_bias_ref.shape[1]
    width = r.act_ref.shape[1]
    atoms = r.act_ref.shape[0] // 3
    tokens = r.table_rows.shape[0] * 2 // (3 * channels)
    tiles = atoms // LANES
    pairs = tokens // 2
    meta = atoms + channels * pairs
    first_valid = jnp.where(index == 0, atoms, 0)
    end_valid = jnp.where(index == count - 1, 2 * atoms, 3 * atoms)
    first_query = 2 * HALO
    even = index % 2 == 0
    copies = [
        pltpu.make_async_copy(own_hbm, r.payload_ref.at[1], r.sems.at[0]),
        pltpu.make_async_copy(near_hbm, r.payload_ref.at[jnp.where(even, 2, 0)], r.sems.at[1]),
    ]
    if far_hbm is not None:
        copies.append(
            pltpu.make_async_copy(far_hbm, r.payload_ref.at[jnp.where(even, 0, 2)], r.sems.at[2])
        )
    small_copies = [
        pltpu.make_async_copy(source, target, r.sems.at[3 + i])
        for i, (source, target) in enumerate(
            zip(small_hbm, (r.w_single_ref, r.w_mlp_ref, r.w_bias_ref))
        )
    ]
    for copy in small_copies + copies:
        copy.start()
    for copy in small_copies:
        copy.wait()

    big = 256
    group = 1 << GROUP_BITS
    select = (iota((big, channels), 0) >> GROUP_BITS == iota((big, channels), 1)).astype(BF16)
    same_query = ((iota((big, big), 0) ^ iota((big, big), 1)) & (group - 1)) == 0
    for layer in range(3):
        by_row = dot_nt(select, r.w_mlp_ref[layer]).astype(BF16)
        r.mlp_ref[layer] = jnp.where(same_query, dot_nt(by_row, select), 0.0).astype(BF16)
    per_block = heads * group
    pick_head = (iota((per_block, heads), 0) >> GROUP_BITS == iota((per_block, heads), 1)).astype(BF16)
    for layer in range(BLOCKS):
        by_row = dot(pick_head, r.w_bias_ref[layer]).astype(BF16)
        r.bias_weight_ref[layer * per_block : (layer + 1) * per_block, :] = jnp.where(
            same_query[0:per_block], dot_nt(by_row, select), 0.0
        ).astype(BF16)

    for copy in copies:
        copy.wait()
    if far_hbm is None:
        absent = jnp.where(even, 0, 2)
        r.payload_ref[absent] = jnp.zeros_like(r.payload_ref[absent])
    sides = tuple(r.payload_ref.at[side] for side in range(3))
    metas = [ref[meta : meta + 16, :].astype(F32) for ref in sides]
    number = iota((3 * tiles, LANES), 0) * LANES + iota((3 * tiles, LANES), 1)
    relative = jnp.concatenate(
        [m[0:tiles] + s for m, s in zip(metas, (-tokens, 0, tokens))], axis=0
    )
    inside = (number >= first_valid) & (number < end_valid)
    relative = jnp.where(inside, relative, -64.0)
    relative_int = relative.astype(jnp.int32)
    offset_lanes = atoms // QB
    offset_row = (
        metas[0][3:4]
        + pltpu.roll(metas[1][3:4], offset_lanes, 1)
        + pltpu.roll(metas[2][3:4], 2 * offset_lanes, 1)
    )
    r.scalars_vmem[...] = jnp.broadcast_to(offset_row, (8, LANES)).astype(jnp.int32)
    copy = pltpu.make_async_copy(r.scalars_vmem, r.scalars, r.sems.at[6])
    copy.start()
    for tile in range(3 * tiles):
        r.token_rows[tile] = jnp.broadcast_to(relative_int[tile : tile + 1], (8, LANES))
    r.token_rows[3 * tiles] = jnp.zeros((8, LANES), jnp.int32)

    eye = iota((LANES, LANES), 0) == iota((LANES, LANES), 1)
    ones = jnp.ones((LANES, LANES), BF16)
    for side, ref in enumerate(sides):
        for tile in range(tiles):
            rows = ref[tile * LANES : (tile + 1) * LANES, :]
            at = side * tiles + tile
            where = slice(at * LANES, (at + 1) * LANES)
            r.act_ref[where, :] = rows.astype(F32)
            r.held_ref[where, :] = (
                (iota((LANES, LANES), 0) + at * LANES >= first_valid)
                & (iota((LANES, LANES), 0) + at * LANES < end_valid)
            ).astype(F32)
            relu = jnp.maximum(rows, jnp.zeros((), BF16))
            r.key_terms[at] = dot_nt(r.w_single_ref[1], relu).astype(BF16).astype(F32)
            column = dot(jnp.where(eye, relative[at : at + 1], 0.0).astype(BF16), ones)
            column = column.astype(jnp.int32)
            base = (column & 1) * (LANES // 2)
            r.token_base[where, :] = base
            r.token_shift[where, :] = LANES // 4 - column
        for pair in range(pairs):
            row = atoms + channels * pair
            to = (side * pairs + pair) * channels
            r.table_rows[to : to + channels, :] = ref[row : row + channels, :].astype(F32)
    r.key_terms[3 * tiles] = jnp.zeros((channels, LANES), F32)

    w_query = jnp.transpose(r.w_single_ref[0].astype(F32))
    window_rows = QB * PAIR_GROUP * groups
    first_row = pl.multiple_of(first_query + QB * first_window, QB)
    for row in range(0, window_rows, QB * PAIR_GROUP):
        where = pl.ds(pl.multiple_of(first_row + row, QB), QB * PAIR_GROUP)
        token = LANES // 4 - r.token_shift[where, :]
        hit = ((token >> 1) == iota(token.shape, 1)).astype(F32).astype(BF16)
        r.left_terms[where, 0:LANES] = hit
        r.left_terms[where, LANES:] = jnp.maximum(r.act_ref[where, :], 0.0).astype(BF16)
    padded = -(-3 * pairs // 16) * 16
    for c in range(channels):
        at = slice(c % 2 * LANES, (c % 2 + 1) * LANES)
        rows = [
            r.table_rows[pl.ds(8 * channels * g + c, 8, stride=channels), :]
            for g in range(3 * pairs // 8)
        ]
        rows.append(jnp.zeros((padded - 3 * pairs, LANES), F32))
        r.right_terms[c // 2, 0:padded, at] = jnp.concatenate(rows, axis=0).astype(BF16)
        r.right_terms[c // 2, padded:LANES, at] = jnp.zeros((LANES - padded, LANES), BF16)
        r.right_terms[c // 2, LANES:, at] = jnp.broadcast_to(
            w_query[:, c : c + 1], (width, LANES)
        ).astype(BF16)

    for c in range(channels // 2):
        band = dot(r.left_terms[pl.ds(first_row, window_rows), :], r.right_terms[c])
        for d in range(2):
            at = slice(d * LANES, (d + 1) * LANES)
            r.band_ref[2 * c + d, pl.ds(first_row, window_rows), :] = band[:, at]

    copy.wait()
    lane = iota((channels, LANES), 1)
    lane8 = iota((8, LANES), 1)
    log2e = math.log2(math.e)

    def window_at(step, w):
        return first_window + step * PAIR_GROUP + w

    def column_stage(step, w):
        n = window_at(step, w)
        query = pl.multiple_of(first_query + QB * n, QB)
        start = key_start(r, n)
        tile = start // LANES
        shift = start % LANES
        back = LANES - shift
        key_tokens = pltpu.roll(
            jnp.where(lane8 >= shift, r.token_rows[tile], r.token_rows[tile + 1]), back, 1
        )
        r.side_ref[w] = pltpu.roll(
            jnp.where(lane >= shift, r.key_terms[tile], r.key_terms[tile + 1]), back, 1
        )
        for g in range(QB // 8):
            rows = pl.ds(query + 8 * g, 8)
            r.column_ref[w, 8 * g : 8 * g + 8, :] = (
                jnp.clip(key_tokens + r.token_shift[rows, :], 0, LANES // 2 - 1)
                + r.token_base[rows, :]
            )

    def start_stage(step, w):
        query = pl.multiple_of(first_query + QB * window_at(step, w), QB)
        slot = step % PAIR_SLOTS
        for g in range(QB // 8):
            half, part = g // (group // 8), g % (group // 8)
            at = slice(half * LANES, (half + 1) * LANES)
            column = r.column_ref[w, 8 * g : 8 * g + 8, :]
            rows = pl.ds(query + 8 * g, 8)
            for e in range(channels):
                row = e * group + 8 * part
                r.start_ref[slot, w, row : row + 8, at] = jnp.take_along_axis(
                    r.band_ref[e, rows, :], column, axis=1, mode="promise_in_bounds"
                ) + jnp.broadcast_to(r.side_ref[w, e : e + 1, :], (8, LANES))

    def relu(values):
        return jnp.maximum(values.astype(BF16), jnp.zeros((), BF16))

    def first_stage(step, w):
        slot = (step + 3) % PAIR_SLOTS
        r.second_ref[w] = relu(dot(r.mlp_ref[0], relu(r.start_ref[slot, w])))

    def second_stage(w):
        r.third_ref[w] = relu(dot(r.mlp_ref[1], r.second_ref[w]))

    def norm_stage(step, w):
        slot = (step + 1) % PAIR_SLOTS
        third = dot(r.mlp_ref[2], r.third_ref[w])
        for half in range(2):
            at = slice(half * LANES, (half + 1) * LANES)
            normed = []
            for part in range(group // 8):
                pair = [
                    third[e * group + 8 * part : e * group + 8 * part + 8, at]
                    + r.start_ref[slot, w, e * group + 8 * part : e * group + 8 * part + 8, at]
                    for e in range(channels)
                ]
                centre = sum(pair[1:], pair[0]) * (1.0 / channels)
                shifted = [p - centre for p in pair]
                spread = sum([s * s for s in shifted[1:]], shifted[0] * shifted[0])
                factor = lax.rsqrt(spread * (1.0 / channels) + EPSILON) * log2e
                normed.append([s * factor for s in shifted])
            for e in range(channels):
                rows = jnp.concatenate([n[e] for n in normed], axis=0)
                r.normed_ref[w, e * group : (e + 1) * group, at] = rows.astype(BF16)

    def bias_stage(step, w):
        to_ref = bias_at((step - PAIR_DEPTH) * PAIR_GROUP + w)
        bias = dot(r.bias_weight_ref[...], r.normed_ref[w])
        for layer in range(BLOCKS):
            part = bias[layer * per_block : (layer + 1) * per_block]
            to_ref[layer, 0:per_block, :] = part[:, 0:LANES]
            to_ref[layer, per_block : 2 * per_block, :] = part[:, LANES:]

    def pair_step(step, carry=None):
        def live(behind):
            return not isinstance(step, int) or 0 <= step - behind < groups

        for w in range(PAIR_GROUP):
            if live(4):
                bias_stage(step, w)
            if live(3):
                norm_stage(step, w)
            if live(2):
                second_stage(w)
            if live(1):
                first_stage(step, w)
            if live(0):
                column_stage(step, w)
                start_stage(step, w)
        return carry

    for step in range(PAIR_DEPTH):
        pair_step(step)
    if groups > PAIR_DEPTH:
        lax.fori_loop(PAIR_DEPTH, groups + jnp.minimum(index, 0), pair_step, 0)
    for step in range(max(groups, PAIR_DEPTH), groups + PAIR_DEPTH):
        pair_step(step)
    return metas, relative_int


def window_split(window_count):
    early = EARLY
    even = lax.rem(shard_place()[0], 2) == 0
    return early, jnp.where(even, window_count - early, 0), jnp.where(even, 0, early)


def early_kernel(own_hbm, near_hbm, w_single_hbm, w_mlp_hbm, w_bias_hbm, out_ref, *scratch):
    r = Refs(PAIR_NAMES, scratch)
    atoms = r.act_ref.shape[0] // 3
    early, first_window, _ = window_split((atoms + 5 * HALO) // QB)
    pair_windows(
        r,
        own_hbm,
        near_hbm,
        None,
        (w_single_hbm, w_mlp_hbm, w_bias_hbm),
        first_window,
        early // PAIR_GROUP,
        lambda n: out_ref.at[n],
    )


def main_kernel(
    own_hbm,
    near_hbm,
    far_hbm,
    early_ref,
    w_single_hbm,
    w_mlp_hbm,
    w_bias_hbm,
    w_attn_hbm,
    w_out_hbm,
    w_in_hbm,
    w_trans_out_hbm,
    w_token_hbm,
    token_out_ref,
    atom_out_ref,
    *scratch,
):
    r = Refs(PAIR_NAMES + MAIN_NAMES, scratch)
    index, count = shard_place()
    atoms, width = atom_out_ref.shape
    tokens = token_out_ref.shape[0]
    heads = r.w_bias_ref.shape[1]
    head_size = width // heads
    tiles = atoms // LANES
    group = QB // 2
    per_block = heads * group
    log2e = math.log2(math.e)
    first_query = 2 * HALO
    window_count = (atoms + 5 * HALO) // QB
    early, early_first, late_first = window_split(window_count)
    even = lax.rem(index, 2) == 0
    weight_copies = [
        pltpu.make_async_copy(source, target, r.weight_sems.at[i])
        for i, (source, target) in enumerate(
            (
                (w_attn_hbm, r.w_attn_ref),
                (w_out_hbm, r.w_out_ref),
                (w_in_hbm, r.w_in_ref),
                (w_trans_out_hbm, r.w_trans_out_ref),
                (w_token_hbm, r.w_token_ref),
            )
        )
    ]
    for copy in weight_copies:
        copy.start()
    metas, relative_int = pair_windows(
        r,
        own_hbm,
        near_hbm,
        far_hbm,
        (w_single_hbm, w_mlp_hbm, w_bias_hbm),
        late_first,
        (window_count - early) // PAIR_GROUP,
        lambda n: r.bias_ref.at[n],
    )
    for copy in weight_copies:
        copy.wait()
    head_of_lane = iota((QB // 2, width), 1) // head_size
    scale = log2e / math.sqrt(head_size)

    def project(layer, first, rows, chunk):
        w_first = jnp.concatenate([r.w_attn_ref[layer, 0], r.w_attn_ref[layer, 1]], axis=1)
        w_second = jnp.concatenate([r.w_attn_ref[layer, 2], r.w_attn_ref[layer, 3]], axis=1)
        for row in range(first, first + rows, chunk):
            where = slice(row, row + chunk)
            normed = normalize(r.act_ref[where, :], 1).astype(BF16)
            held = r.held_ref[where, :] > 0.0
            both = dot(normed, w_first)
            r.query_ref[where, :] = (both[:, :width] * scale).astype(BF16)
            r.key_ref[where, :] = jnp.where(held, both[:, width:], 0.0)
            both = dot(normed, w_second)
            r.value_ref[where, :] = jnp.where(held, both[:, :width], 0.0)
            r.gate_ref[where, :] = jax.nn.sigmoid(both[:, width:])

    def attend(layer, n, bias):
        query = pl.multiple_of(first_query + QB * n, QB)
        start = key_start(r, n)
        q = r.query_ref[pl.ds(query, QB), :]
        k = r.key_ref[pl.ds(start, KW), :].astype(BF16)
        v = jnp.concatenate(
            [r.value_ref[pl.ds(start, KW), :], r.held_ref[pl.ds(start, KW), :]], axis=1
        ).astype(BF16)
        blocks = []
        for half in range(2):
            part = q[half * QB // 2 : (half + 1) * QB // 2]
            for h in range(heads):
                blocks.append(jnp.where(head_of_lane == h, part, jnp.zeros((), BF16)))
        scores = dot_nt(jnp.concatenate(blocks, axis=0), k) + bias
        sums = dot(jnp.exp2(scores).astype(BF16), v)
        halves = []
        for half in range(2):
            base = half * per_block
            value = sums[base : base + group, :LANES]
            total = sums[base : base + group, LANES:]
            for h in range(1, heads):
                row = base + h * group
                value = jnp.where(head_of_lane == h, sums[row : row + group, :LANES], value)
                total = jnp.where(head_of_lane == h, sums[row : row + group, LANES:], total)
            halves.append(value / total)
        attended = jnp.concatenate(halves, axis=0)
        r.gated_ref[pl.ds(query, QB), :] = (attended * r.gate_ref[pl.ds(query, QB), :]).astype(BF16)

    def dense(layer, first, rows, chunk):
        for row in range(first, first + rows, chunk):
            where = slice(row, row + chunk)
            act = r.act_ref[where, :] + dot(r.gated_ref[where, :], r.w_out_ref[layer])
            act = jnp.where(r.held_ref[where, :] > 0.0, act, 0.0)
            normed = normalize(act, 1).astype(BF16)
            gate_part = dot(normed, r.w_in_ref[layer, 0])
            up_part = dot(normed, r.w_in_ref[layer, 1])
            hidden = (gate_part / (1.0 + jnp.exp(-gate_part)) * up_part).astype(BF16)
            r.act_ref[where, :] = act + dot(hidden, r.w_trans_out_ref[layer])

    chunk_of = (864, 672, 480)
    for layer in range(BLOCKS):
        first_window = layer * HALO // QB
        last_window = window_count - layer * HALO // QB
        windows = last_window - first_window
        query_first = first_query + QB * first_window
        query_rows = QB * windows
        key_first = query_first - HALO
        key_rows = query_rows + 2 * HALO
        project(layer, key_first, key_rows, key_rows // 3)

        skipped = layer * HALO // QB
        from_early = jnp.where(even, 0, skipped)
        from_late = jnp.where(even, skipped, 0)
        for w in range(early - skipped):
            n = from_early + w
            attend(layer, early_first + n, early_ref[n, layer])
        for w in range(window_count - early - skipped):
            n = from_late + w
            attend(layer, late_first + n, r.bias_ref[n, layer])
        dense(layer, query_first, query_rows, chunk_of[layer])

    atom_out_ref[...] = r.act_ref[atoms : 2 * atoms, :].astype(BF16)
    reach = atoms + LANES
    r.feature_ref[atoms + HALO : reach, :] = jnp.zeros_like(r.feature_ref[atoms + HALO : reach, :])
    for row in range(0, atoms + HALO, 160):
        rows = r.act_ref[atoms + row : atoms + row + 160, :].astype(BF16)
        features = jnp.maximum(dot(rows, r.w_token_ref[...]), 0.0)
        r.feature_ref[row : row + 160, :] = features.astype(BF16)
    slot = iota((tokens, LANES), 0) + tokens
    member = jnp.concatenate(
        [
            (slot == relative_int[tile : tile + 1]).astype(F32)
            for tile in range(tiles, 2 * tiles + 1)
        ],
        axis=1,
    ).astype(BF16)
    sums = dot(member, r.feature_ref[...])
    diagonal = (iota((tokens, LANES), 0) == iota((tokens, LANES), 1)).astype(F32)
    atoms_of = jnp.sum(diagonal * metas[1][4:5], axis=1, keepdims=True)
    token_out_ref[...] = (sums / atoms_of).astype(BF16)


def shards(
    atom_single,
    atom_token,
    token_atoms,
    window_offset,
    token_pair,
    w_zpair,
    w_single,
    w_pair_mlp,
    w_bias,
    w_attn,
    w_out,
    w_trans_in,
    w_trans_out,
    w_token,
):
    index, count = shard_place()
    atoms, width = atom_single.shape
    tokens, band, depth = token_pair.shape
    channels = w_zpair.shape[1]
    tiles = atoms // LANES
    pairs = tokens * band // LANES
    payload_rows = atoms + channels * pairs + 16

    vmem = pl.BlockSpec(memory_space=pltpu.VMEM)
    anywhere = pl.BlockSpec(memory_space=pl.ANY)
    parts = 3
    payload = pl.pallas_call(
        project_kernel,
        out_shape=jax.ShapeDtypeStruct((payload_rows, width), BF16),
        in_specs=[anywhere] * 6,
        out_specs=anywhere,
        scratch_shapes=[
            pltpu.VMEM((tokens * band, depth), BF16),
            pltpu.VMEM((channels, depth), BF16),
            pltpu.VMEM((atoms,), jnp.int32),
            pltpu.VMEM((tokens,), jnp.int32),
            pltpu.VMEM(window_offset.shape, jnp.int32),
            pltpu.VMEM((payload_rows - atoms, width), BF16),
            pltpu.VMEM((16, width), F32),
            pltpu.SemaphoreType.DMA((4,)),
            pltpu.SemaphoreType.DMA((parts,)),
            pltpu.SemaphoreType.DMA((parts + 1,)),
        ],
        name="project",
    )(
        token_pair.reshape(tokens * band, depth),
        jnp.swapaxes(w_zpair, 0, 1),
        atom_single,
        atom_token,
        token_atoms,
        window_offset,
    )
    near = [(i, i ^ 1) for i in range(count)]
    far = [(i, ((i + 1) ^ 1) - 1) for i in range(1, count - 1)]
    first_side = lax.ppermute(payload, RING, near)
    second_side = lax.ppermute(payload, RING, far)

    in_hbm = pl.BlockSpec(memory_space=pltpu.HBM)
    small = (
        jnp.swapaxes(w_single, 1, 2),
        w_pair_mlp,
        jnp.swapaxes(w_bias, 1, 2),
    )
    large = (w_attn, w_out, w_trans_in, w_trans_out, w_token)
    reach = 3 * atoms
    windows = (atoms + 5 * HALO) // QB
    early, _, _ = window_split(windows)
    heads = w_bias.shape[2]
    channels_out = w_token.shape[1]

    def hbm(*arrays):
        return [pltpu.with_memory_space_constraint(x, pltpu.HBM) for x in arrays]

    pair_scratch = [
        pltpu.VMEM((3, payload_rows, width), BF16),
        *[pltpu.VMEM(w.shape, BF16) for w in small],
        pltpu.VMEM((8, LANES), jnp.int32),
        pltpu.SMEM((8, LANES), jnp.int32),
        pltpu.VMEM((3 * tiles + 1, 8, LANES), jnp.int32),
        pltpu.VMEM((3 * tiles + 1, channels, LANES), F32),
        pltpu.VMEM((reach, LANES), jnp.int32),
        pltpu.VMEM((reach, LANES), jnp.int32),
        pltpu.VMEM((3 * pairs * channels, LANES), F32),
        pltpu.VMEM((channels, reach, LANES), F32),
        pltpu.VMEM((PAIR_GROUP, channels, LANES), F32),
        pltpu.VMEM((PAIR_GROUP, QB, LANES), jnp.int32),
        pltpu.VMEM((PAIR_SLOTS, PAIR_GROUP, 256, 256), F32),
        *[pltpu.VMEM((PAIR_GROUP, 256, 256), BF16)] * 3,
        pltpu.VMEM((reach, 256), BF16),
        pltpu.VMEM((channels // 2, 256, 256), BF16),
        pltpu.VMEM((3, 256, 256), BF16),
        pltpu.VMEM((BLOCKS * heads * 256 // channels, 256), BF16),
        pltpu.VMEM((reach, width), F32),
        pltpu.VMEM((reach, LANES), F32),
        pltpu.SemaphoreType.DMA((7,)),
    ]
    early_bias = pl.pallas_call(
        early_kernel,
        out_shape=jax.ShapeDtypeStruct((early, BLOCKS, heads * QB, KW), F32),
        in_specs=[in_hbm, anywhere] + [in_hbm] * len(small),
        out_specs=vmem,
        scratch_shapes=pair_scratch,
        compiler_params=pltpu.CompilerParams(vmem_limit_bytes=40 * 2**20),
        cost_estimate=pl.CostEstimate(
            flops=2 * 10**9, transcendentals=10**5, bytes_accessed=8 * 10**6
        ),
        name="early_pairs",
    )(*hbm(payload), first_side, *hbm(*small))
    token_single, atom_out = pl.pallas_call(
        main_kernel,
        out_shape=(
            jax.ShapeDtypeStruct((tokens, channels_out), BF16),
            jax.ShapeDtypeStruct((atoms, width), BF16),
        ),
        in_specs=[in_hbm] + [anywhere] * 2 + [vmem] + [in_hbm] * (len(small) + len(large)),
        out_specs=(vmem, vmem),
        scratch_shapes=pair_scratch
        + [
            *[pltpu.VMEM(w.shape, BF16) for w in large],
            pltpu.VMEM((windows - early, BLOCKS, heads * QB, KW), F32),
            pltpu.VMEM((reach, width), BF16),
            pltpu.VMEM((reach, width), F32),
            pltpu.VMEM((reach, width), F32),
            pltpu.VMEM((reach, width), F32),
            pltpu.VMEM((reach, width), BF16),
            pltpu.VMEM((atoms + LANES, channels_out), BF16),
            pltpu.SemaphoreType.DMA((len(large),)),
        ],
        compiler_params=pltpu.CompilerParams(vmem_limit_bytes=48 * 2**20),
        name="encode",
    )(*hbm(payload), first_side, second_side, early_bias, *hbm(*small, *large))
    return token_single, atom_out


def solution(mesh):
    split = ("group", "seq", "chan", "sub")
    in_specs = (
        P(split, None),
        P(split),
        P(split),
        P(split),
        P(split, None, None),
        P(),
        P(),
        P(),
        P(),
        P(),
        P(),
        P(),
        P(),
        P(),
    )
    out_specs = (P(split, None), P(split, None))
    return jax.shard_map(shards, mesh=mesh, in_specs=in_specs, out_specs=out_specs, check_vma=False)
```

```python
import math

import jax
import jax.numpy as jnp
from jax import lax
from jax.experimental import pallas as pl
from jax.experimental.pallas import tpu as pltpu
from jax.sharding import PartitionSpec as P

BLOCKS = 3
QB = 32
KW = 128
HALO = 96
LANES = 128
PAIR_DEPTH = 4
PAIR_SLOTS = 4
PAIR_GROUP = 3
GROUP_BITS = 4
EARLY = 15
EPSILON = 1e-05
RING = ("seq", "chan", "sub")
NT = (((1,), (1,)), ((), ()))
F32 = jnp.float32
BF16 = jnp.bfloat16


def dot(a, b):
    return jnp.dot(a, b, preferred_element_type=F32)


def dot_nt(a, b):
    return lax.dot_general(a, b, NT, preferred_element_type=F32)


def iota(shape, axis):
    return lax.broadcasted_iota(jnp.int32, shape, axis)


def shard_place():
    index, count = 0, 1
    for name in RING:
        index = index * lax.axis_size(name) + lax.axis_index(name)
        count = count * lax.axis_size(name)
    return index, count


def normalize(values, axis):
    centre = jnp.mean(values, axis=axis, keepdims=True)
    shifted = values - centre
    spread = jnp.mean(shifted * shifted, axis=axis, keepdims=True)
    return shifted * lax.rsqrt(spread + EPSILON)


def project_kernel(
    pair_hbm,
    wz_hbm,
    atom_hbm,
    token_hbm,
    atoms_of_hbm,
    offset_hbm,
    out_hbm,
    pair_ref,
    wz_ref,
    token_ref,
    atoms_of_ref,
    offset_ref,
    band_ref,
    meta_ref,
    small_sems,
    in_sems,
    out_sems,
):
    rows, width = pair_ref.shape
    atoms = atom_hbm.shape[0]
    tokens = atoms_of_hbm.shape[0]
    channels = wz_hbm.shape[0]
    tiles = atoms // LANES
    parts = in_sems.shape[0]
    step = rows // parts
    band_step = channels * step // LANES
    meta = atoms + channels * rows // LANES

    loads = [
        pltpu.make_async_copy(
            pair_hbm.at[pl.ds(step * part, step)],
            pair_ref.at[pl.ds(step * part, step)],
            in_sems.at[part],
        )
        for part in range(parts)
    ]
    small = [
        pltpu.make_async_copy(wz_hbm, wz_ref, small_sems.at[0]),
        pltpu.make_async_copy(token_hbm, token_ref, small_sems.at[1]),
        pltpu.make_async_copy(atoms_of_hbm, atoms_of_ref, small_sems.at[2]),
        pltpu.make_async_copy(offset_hbm, offset_ref, small_sems.at[3]),
    ]
    atom_copy = pltpu.make_async_copy(atom_hbm, out_hbm.at[pl.ds(0, atoms)], out_sems.at[parts])
    loads[0].start()
    for copy in small + loads[1:]:
        copy.start()
    atom_copy.start()

    eye = iota((width, width), 0) == iota((width, width), 1)
    centring = (eye.astype(F32) - 1.0 / width).astype(BF16)
    average = jnp.full((channels, width), 1.0 / width, BF16)
    for copy in small:
        copy.wait()
    index, _ = shard_place()
    meta_ref[...] = jnp.zeros_like(meta_ref)
    base = (index - 1) * tokens
    for tile in range(tiles):
        local = token_ref[LANES * tile : LANES * (tile + 1)].reshape(1, LANES) - base
        meta_ref[tile : tile + 1, :] = local.astype(F32)
    meta_ref[tiles : tiles + 1, 0 : offset_ref.shape[0]] = (
        offset_ref[...].reshape(1, offset_ref.shape[0]).astype(F32)
    )
    meta_ref[tiles + 1 : tiles + 2, 0:tokens] = (
        atoms_of_ref[...].reshape(1, tokens).astype(F32)
    )
    band_ref[meta - atoms :, :] = meta_ref[...].astype(BF16)
    stores = []
    for part in range(parts):
        loads[part].wait()
        shifted = dot(pair_ref[step * part : step * (part + 1), :], centring)
        spread = dot_nt(average, (shifted * shifted).astype(BF16))
        projected = dot_nt(wz_ref[...], shifted.astype(BF16))
        projected = (projected * lax.rsqrt(spread + EPSILON)).astype(BF16)
        for tile in range(step // LANES):
            row = band_step * part + channels * tile
            band_ref[row : row + channels, :] = projected[:, LANES * tile : LANES * (tile + 1)]
        first, count = band_step * part, band_step + (16 if part == parts - 1 else 0)
        copy = pltpu.make_async_copy(
            band_ref.at[pl.ds(first, count)],
            out_hbm.at[pl.ds(atoms + first, count)],
            out_sems.at[part],
        )
        copy.start()
        stores.append(copy)
    for copy in stores:
        copy.wait()
    atom_copy.wait()


class Refs:
    def __init__(self, names, refs):
        self.__dict__.update(zip(names, refs))


PAIR_NAMES = (
    "payload_ref",
    "w_single_ref",
    "w_mlp_ref",
    "w_bias_ref",
    "scalars_vmem",
    "scalars",
    "token_rows",
    "key_terms",
    "token_shift",
    "token_base",
    "table_rows",
    "band_ref",
    "side_ref",
    "column_ref",
    "start_ref",
    "second_ref",
    "third_ref",
    "normed_ref",
    "left_terms",
    "right_terms",
    "mlp_ref",
    "bias_weight_ref",
    "act_ref",
    "held_ref",
    "sems",
)
MAIN_NAMES = (
    "w_attn_ref",
    "w_out_ref",
    "w_in_ref",
    "w_trans_out_ref",
    "w_token_ref",
    "bias_ref",
    "query_ref",
    "gate_ref",
    "key_ref",
    "value_ref",
    "gated_ref",
    "feature_ref",
    "weight_sems",
)


def key_start(r, n):
    offset_lanes = r.act_ref.shape[0] // 3 // QB
    return HALO + QB * n + r.scalars[0, n + offset_lanes - 2 * HALO // QB]


def pair_windows(r, own_hbm, near_hbm, far_hbm, small_hbm, first_window, groups, bias_at, later=()):
    index, count = shard_place()
    channels = r.w_mlp_ref.shape[1]
    heads = r.w_bias_ref.shape[1]
    width = r.act_ref.shape[1]
    atoms = r.act_ref.shape[0] // 3
    tokens = r.table_rows.shape[0] * 2 // (3 * channels)
    tiles = atoms // LANES
    pairs = tokens // 2
    meta = atoms + channels * pairs
    first_valid = jnp.where(index == 0, atoms, 0)
    end_valid = jnp.where(index == count - 1, 2 * atoms, 3 * atoms)
    first_query = 2 * HALO
    even = index % 2 == 0
    copies = [
        pltpu.make_async_copy(own_hbm, r.payload_ref.at[1], r.sems.at[0]),
        pltpu.make_async_copy(near_hbm, r.payload_ref.at[jnp.where(even, 2, 0)], r.sems.at[1]),
    ]
    if far_hbm is not None:
        copies.append(
            pltpu.make_async_copy(far_hbm, r.payload_ref.at[jnp.where(even, 0, 2)], r.sems.at[2])
        )
    small_copies = [
        pltpu.make_async_copy(source, target, r.sems.at[3 + i])
        for i, (source, target) in enumerate(
            zip(small_hbm, (r.w_single_ref, r.w_mlp_ref, r.w_bias_ref))
        )
    ]
    for copy in (*small_copies, *copies, *later):
        copy.start()
    for copy in small_copies:
        copy.wait()

    big = 256
    group = 1 << GROUP_BITS
    select = (iota((big, channels), 0) >> GROUP_BITS == iota((big, channels), 1)).astype(BF16)
    same_query = ((iota((big, big), 0) ^ iota((big, big), 1)) & (group - 1)) == 0
    for layer in range(3):
        by_row = dot_nt(select, r.w_mlp_ref[layer]).astype(BF16)
        r.mlp_ref[layer] = jnp.where(same_query, dot_nt(by_row, select), 0.0).astype(BF16)
    per_block = heads * group
    pick_head = (iota((per_block, heads), 0) >> GROUP_BITS == iota((per_block, heads), 1)).astype(BF16)
    for layer in range(BLOCKS):
        by_row = dot(pick_head, r.w_bias_ref[layer]).astype(BF16)
        r.bias_weight_ref[layer * per_block : (layer + 1) * per_block, :] = jnp.where(
            same_query[0:per_block], dot_nt(by_row, select), 0.0
        ).astype(BF16)

    for copy in copies:
        copy.wait()
    if far_hbm is None:
        absent = jnp.where(even, 0, 2)
        r.payload_ref[absent] = jnp.zeros_like(r.payload_ref[absent])
    sides = tuple(r.payload_ref.at[side] for side in range(3))
    metas = [ref[meta : meta + 16, :].astype(F32) for ref in sides]
    number = iota((3 * tiles, LANES), 0) * LANES + iota((3 * tiles, LANES), 1)
    relative = jnp.concatenate(
        [m[0:tiles] + s for m, s in zip(metas, (-tokens, 0, tokens))], axis=0
    )
    inside = (number >= first_valid) & (number < end_valid)
    relative = jnp.where(inside, relative, -64.0)
    relative_int = relative.astype(jnp.int32)
    offset_lanes = atoms // QB
    offset_row = (
        metas[0][3:4]
        + pltpu.roll(metas[1][3:4], offset_lanes, 1)
        + pltpu.roll(metas[2][3:4], 2 * offset_lanes, 1)
    )
    r.scalars_vmem[...] = jnp.broadcast_to(offset_row, (8, LANES)).astype(jnp.int32)
    copy = pltpu.make_async_copy(r.scalars_vmem, r.scalars, r.sems.at[6])
    copy.start()
    for tile in range(3 * tiles):
        r.token_rows[tile] = jnp.broadcast_to(relative_int[tile : tile + 1], (8, LANES))
    r.token_rows[3 * tiles] = jnp.zeros((8, LANES), jnp.int32)

    eye = iota((LANES, LANES), 0) == iota((LANES, LANES), 1)
    ones = jnp.ones((LANES, LANES), BF16)
    for side, ref in enumerate(sides):
        for tile in range(tiles):
            rows = ref[tile * LANES : (tile + 1) * LANES, :]
            at = side * tiles + tile
            where = slice(at * LANES, (at + 1) * LANES)
            r.act_ref[where, :] = rows.astype(F32)
            if far_hbm is not None:
                r.held_ref[where, :] = (
                    (iota((LANES, LANES), 0) + at * LANES >= first_valid)
                    & (iota((LANES, LANES), 0) + at * LANES < end_valid)
                ).astype(F32)
            relu = jnp.maximum(rows, jnp.zeros((), BF16))
            r.key_terms[at] = dot_nt(r.w_single_ref[1], relu).astype(BF16).astype(F32)
            column = dot(jnp.where(eye, relative[at : at + 1], 0.0).astype(BF16), ones)
            column = column.astype(jnp.int32)
            base = (column & 1) * (LANES // 2)
            r.token_base[where, :] = base
            r.token_shift[where, :] = LANES // 4 - column
        for pair in range(pairs):
            row = atoms + channels * pair
            to = (side * pairs + pair) * channels
            r.table_rows[to : to + channels, :] = ref[row : row + channels, :].astype(F32)
    r.key_terms[3 * tiles] = jnp.zeros((channels, LANES), F32)

    w_query = jnp.transpose(r.w_single_ref[0].astype(F32))
    window_rows = QB * PAIR_GROUP * groups
    first_row = pl.multiple_of(first_query + QB * first_window, QB)
    for row in range(0, window_rows, QB * PAIR_GROUP):
        where = pl.ds(pl.multiple_of(first_row + row, QB), QB * PAIR_GROUP)
        token = LANES // 4 - r.token_shift[where, :]
        hit = ((token >> 1) == iota(token.shape, 1)).astype(F32).astype(BF16)
        r.left_terms[where, 0:LANES] = hit
        r.left_terms[where, LANES:] = jnp.maximum(r.act_ref[where, :], 0.0).astype(BF16)
    padded = -(-3 * pairs // 16) * 16
    for c in range(channels):
        at = slice(c % 2 * LANES, (c % 2 + 1) * LANES)
        rows = [
            r.table_rows[pl.ds(8 * channels * g + c, 8, stride=channels), :]
            for g in range(3 * pairs // 8)
        ]
        rows.append(jnp.zeros((padded - 3 * pairs, LANES), F32))
        r.right_terms[c // 2, 0:padded, at] = jnp.concatenate(rows, axis=0).astype(BF16)
        r.right_terms[c // 2, padded:LANES, at] = jnp.zeros((LANES - padded, LANES), BF16)
        r.right_terms[c // 2, LANES:, at] = jnp.broadcast_to(
            w_query[:, c : c + 1], (width, LANES)
        ).astype(BF16)

    for c in range(channels // 2):
        band = dot(r.left_terms[pl.ds(first_row, window_rows), :], r.right_terms[c])
        for d in range(2):
            at = slice(d * LANES, (d + 1) * LANES)
            r.band_ref[2 * c + d, pl.ds(first_row, window_rows), :] = band[:, at]

    copy.wait()
    lane = iota((channels, LANES), 1)
    lane8 = iota((8, LANES), 1)
    log2e = math.log2(math.e)

    def window_at(step, w):
        return first_window + step * PAIR_GROUP + w

    def column_stage(step, w):
        n = window_at(step, w)
        query = pl.multiple_of(first_query + QB * n, QB)
        start = key_start(r, n)
        tile = start // LANES
        shift = start % LANES
        back = LANES - shift
        key_tokens = pltpu.roll(
            jnp.where(lane8 >= shift, r.token_rows[tile], r.token_rows[tile + 1]), back, 1
        )
        r.side_ref[w] = pltpu.roll(
            jnp.where(lane >= shift, r.key_terms[tile], r.key_terms[tile + 1]), back, 1
        )
        for g in range(QB // 8):
            rows = pl.ds(query + 8 * g, 8)
            r.column_ref[w, 8 * g : 8 * g + 8, :] = (
                jnp.clip(key_tokens + r.token_shift[rows, :], 0, LANES // 2 - 1)
                + r.token_base[rows, :]
            )

    def start_stage(step, w):
        query = pl.multiple_of(first_query + QB * window_at(step, w), QB)
        slot = step % PAIR_SLOTS
        for g in range(QB // 8):
            half, part = g // (group // 8), g % (group // 8)
            at = slice(half * LANES, (half + 1) * LANES)
            column = r.column_ref[w, 8 * g : 8 * g + 8, :]
            rows = pl.ds(query + 8 * g, 8)
            for e in range(channels):
                row = e * group + 8 * part
                r.start_ref[slot, w, row : row + 8, at] = jnp.take_along_axis(
                    r.band_ref[e, rows, :], column, axis=1, mode="promise_in_bounds"
                ) + jnp.broadcast_to(r.side_ref[w, e : e + 1, :], (8, LANES))

    def relu(values):
        return jnp.maximum(values.astype(BF16), jnp.zeros((), BF16))

    def first_stage(step, w):
        slot = (step + 3) % PAIR_SLOTS
        r.second_ref[w] = relu(dot(r.mlp_ref[0], relu(r.start_ref[slot, w])))

    def second_stage(w):
        r.third_ref[w] = relu(dot(r.mlp_ref[1], r.second_ref[w]))

    def norm_stage(step, w):
        slot = (step + 1) % PAIR_SLOTS
        third = dot(r.mlp_ref[2], r.third_ref[w])
        for half in range(2):
            at = slice(half * LANES, (half + 1) * LANES)
            normed = []
            for part in range(group // 8):
                pair = [
                    third[e * group + 8 * part : e * group + 8 * part + 8, at]
                    + r.start_ref[slot, w, e * group + 8 * part : e * group + 8 * part + 8, at]
                    for e in range(channels)
                ]
                centre = sum(pair[1:], pair[0]) * (1.0 / channels)
                shifted = [p - centre for p in pair]
                spread = sum([s * s for s in shifted[1:]], shifted[0] * shifted[0])
                factor = lax.rsqrt(spread * (1.0 / channels) + EPSILON) * log2e
                normed.append([s * factor for s in shifted])
            for e in range(channels):
                rows = jnp.concatenate([n[e] for n in normed], axis=0)
                r.normed_ref[w, e * group : (e + 1) * group, at] = rows.astype(BF16)

    def bias_stage(step, w):
        to_ref = bias_at((step - PAIR_DEPTH) * PAIR_GROUP + w)
        bias = dot(r.bias_weight_ref[...], r.normed_ref[w])
        for layer in range(BLOCKS):
            part = bias[layer * per_block : (layer + 1) * per_block]
            to_ref[layer, 0:per_block, :] = part[:, 0:LANES]
            to_ref[layer, per_block : 2 * per_block, :] = part[:, LANES:]

    def pair_step(step, carry=None):
        def live(behind):
            return not isinstance(step, int) or 0 <= step - behind < groups

        for w in range(PAIR_GROUP):
            if live(4):
                bias_stage(step, w)
            if live(3):
                norm_stage(step, w)
            if live(2):
                second_stage(w)
            if live(1):
                first_stage(step, w)
            if live(0):
                column_stage(step, w)
                start_stage(step, w)
        return carry

    for step in range(PAIR_DEPTH):
        pair_step(step)
    if groups > PAIR_DEPTH:
        lax.fori_loop(PAIR_DEPTH, groups + jnp.minimum(index, 0), pair_step, 0)
    for step in range(max(groups, PAIR_DEPTH), groups + PAIR_DEPTH):
        pair_step(step)
    return metas, relative_int


def window_split(window_count):
    early = EARLY
    even = lax.rem(shard_place()[0], 2) == 0
    return early, jnp.where(even, window_count - early, 0), jnp.where(even, 0, early)


def early_kernel(own_hbm, near_hbm, w_single_hbm, w_mlp_hbm, w_bias_hbm, out_ref, *scratch):
    r = Refs(PAIR_NAMES, scratch)
    atoms = r.act_ref.shape[0] // 3
    early, first_window, _ = window_split((atoms + 5 * HALO) // QB)
    pair_windows(
        r,
        own_hbm,
        near_hbm,
        None,
        (w_single_hbm, w_mlp_hbm, w_bias_hbm),
        first_window,
        early // PAIR_GROUP,
        lambda n: out_ref.at[n],
    )


def main_kernel(
    own_hbm,
    near_hbm,
    far_hbm,
    early_ref,
    w_single_hbm,
    w_mlp_hbm,
    w_bias_hbm,
    w_attn_hbm,
    w_out_hbm,
    w_in_hbm,
    w_trans_out_hbm,
    w_token_hbm,
    token_out_ref,
    atom_out_ref,
    *scratch,
):
    r = Refs(PAIR_NAMES + MAIN_NAMES, scratch)
    index, count = shard_place()
    atoms, width = atom_out_ref.shape
    tokens = token_out_ref.shape[0]
    heads = r.w_bias_ref.shape[1]
    head_size = width // heads
    tiles = atoms // LANES
    group = QB // 2
    per_block = heads * group
    log2e = math.log2(math.e)
    first_query = 2 * HALO
    window_count = (atoms + 5 * HALO) // QB
    early, early_first, late_first = window_split(window_count)
    even = lax.rem(index, 2) == 0
    weight_copies = [
        pltpu.make_async_copy(source, target, r.weight_sems.at[i])
        for i, (source, target) in enumerate(
            (
                (w_attn_hbm, r.w_attn_ref),
                (w_out_hbm, r.w_out_ref),
                (w_in_hbm, r.w_in_ref),
                (w_trans_out_hbm, r.w_trans_out_ref),
                (w_token_hbm, r.w_token_ref),
            )
        )
    ]
    metas, relative_int = pair_windows(
        r,
        own_hbm,
        near_hbm,
        far_hbm,
        (w_single_hbm, w_mlp_hbm, w_bias_hbm),
        late_first,
        (window_count - early) // PAIR_GROUP,
        lambda n: r.bias_ref.at[n],
        weight_copies,
    )
    for copy in weight_copies:
        copy.wait()
    head_of_lane = iota((QB // 2, width), 1) // head_size
    scale = log2e / math.sqrt(head_size)

    def project(layer, first, rows, chunk):
        w_first = jnp.concatenate([r.w_attn_ref[layer, 0], r.w_attn_ref[layer, 1]], axis=1)
        w_second = jnp.concatenate([r.w_attn_ref[layer, 2], r.w_attn_ref[layer, 3]], axis=1)
        for row in range(first, first + rows, chunk):
            where = slice(row, row + chunk)
            normed = normalize(r.act_ref[where, :], 1).astype(BF16)
            held = r.held_ref[where, :] > 0.0
            both = dot(normed, w_first)
            r.query_ref[where, :] = (both[:, :width] * scale).astype(BF16)
            r.key_ref[where, :] = jnp.where(held, both[:, width:], 0.0)
            both = dot(normed, w_second)
            r.value_ref[where, :] = jnp.where(held, both[:, :width], 0.0)
            r.gate_ref[where, :] = jax.nn.sigmoid(both[:, width:])

    def attend(layer, n, bias):
        query = pl.multiple_of(first_query + QB * n, QB)
        start = key_start(r, n)
        q = r.query_ref[pl.ds(query, QB), :]
        k = r.key_ref[pl.ds(start, KW), :].astype(BF16)
        v = jnp.concatenate(
            [r.value_ref[pl.ds(start, KW), :], r.held_ref[pl.ds(start, KW), :]], axis=1
        ).astype(BF16)
        blocks = []
        for half in range(2):
            part = q[half * QB // 2 : (half + 1) * QB // 2]
            for h in range(heads):
                blocks.append(jnp.where(head_of_lane == h, part, jnp.zeros((), BF16)))
        scores = dot_nt(jnp.concatenate(blocks, axis=0), k) + bias
        sums = dot(jnp.exp2(scores).astype(BF16), v)
        halves = []
        for half in range(2):
            base = half * per_block
            value = sums[base : base + group, :LANES]
            total = sums[base : base + group, LANES:]
            for h in range(1, heads):
                row = base + h * group
                value = jnp.where(head_of_lane == h, sums[row : row + group, :LANES], value)
                total = jnp.where(head_of_lane == h, sums[row : row + group, LANES:], total)
            halves.append(value / total)
        attended = jnp.concatenate(halves, axis=0)
        r.gated_ref[pl.ds(query, QB), :] = (attended * r.gate_ref[pl.ds(query, QB), :]).astype(BF16)

    def dense(layer, first, rows, chunk):
        for row in range(first, first + rows, chunk):
            where = slice(row, row + chunk)
            act = r.act_ref[where, :] + dot(r.gated_ref[where, :], r.w_out_ref[layer])
            act = jnp.where(r.held_ref[where, :] > 0.0, act, 0.0)
            normed = normalize(act, 1).astype(BF16)
            gate_part = dot(normed, r.w_in_ref[layer, 0])
            up_part = dot(normed, r.w_in_ref[layer, 1])
            hidden = (gate_part / (1.0 + jnp.exp(-gate_part)) * up_part).astype(BF16)
            r.act_ref[where, :] = act + dot(hidden, r.w_trans_out_ref[layer])

    chunk_of = (864, 672, 480)
    for layer in range(BLOCKS):
        first_window = layer * HALO // QB
        last_window = window_count - layer * HALO // QB
        windows = last_window - first_window
        query_first = first_query + QB * first_window
        query_rows = QB * windows
        key_first = query_first - HALO
        key_rows = query_rows + 2 * HALO
        project(layer, key_first, key_rows, key_rows // 3)

        skipped = layer * HALO // QB
        from_early = jnp.where(even, 0, skipped)
        from_late = jnp.where(even, skipped, 0)
        for w in range(early - skipped):
            n = from_early + w
            attend(layer, early_first + n, early_ref[n, layer])
        for w in range(window_count - early - skipped):
            n = from_late + w
            attend(layer, late_first + n, r.bias_ref[n, layer])
        dense(layer, query_first, query_rows, chunk_of[layer])

    atom_out_ref[...] = r.act_ref[atoms : 2 * atoms, :].astype(BF16)
    reach = atoms + LANES
    r.feature_ref[atoms + HALO : reach, :] = jnp.zeros_like(r.feature_ref[atoms + HALO : reach, :])
    for row in range(0, atoms + HALO, 160):
        rows = r.act_ref[atoms + row : atoms + row + 160, :].astype(BF16)
        features = jnp.maximum(dot(rows, r.w_token_ref[...]), 0.0)
        r.feature_ref[row : row + 160, :] = features.astype(BF16)
    slot = iota((tokens, LANES), 0) + tokens
    member = jnp.concatenate(
        [
            (slot == relative_int[tile : tile + 1]).astype(F32)
            for tile in range(tiles, 2 * tiles + 1)
        ],
        axis=1,
    ).astype(BF16)
    sums = dot(member, r.feature_ref[...])
    diagonal = (iota((tokens, LANES), 0) == iota((tokens, LANES), 1)).astype(F32)
    atoms_of = jnp.sum(diagonal * metas[1][4:5], axis=1, keepdims=True)
    token_out_ref[...] = (sums / atoms_of).astype(BF16)


def shards(
    atom_single,
    atom_token,
    token_atoms,
    window_offset,
    token_pair,
    w_zpair,
    w_single,
    w_pair_mlp,
    w_bias,
    w_attn,
    w_out,
    w_trans_in,
    w_trans_out,
    w_token,
):
    index, count = shard_place()
    atoms, width = atom_single.shape
    tokens, band, depth = token_pair.shape
    channels = w_zpair.shape[1]
    tiles = atoms // LANES
    pairs = tokens * band // LANES
    payload_rows = atoms + channels * pairs + 16

    vmem = pl.BlockSpec(memory_space=pltpu.VMEM)
    anywhere = pl.BlockSpec(memory_space=pl.ANY)
    parts = 3
    payload = pl.pallas_call(
        project_kernel,
        out_shape=jax.ShapeDtypeStruct((payload_rows, width), BF16),
        in_specs=[anywhere] * 6,
        out_specs=anywhere,
        scratch_shapes=[
            pltpu.VMEM((tokens * band, depth), BF16),
            pltpu.VMEM((channels, depth), BF16),
            pltpu.VMEM((atoms,), jnp.int32),
            pltpu.VMEM((tokens,), jnp.int32),
            pltpu.VMEM(window_offset.shape, jnp.int32),
            pltpu.VMEM((payload_rows - atoms, width), BF16),
            pltpu.VMEM((16, width), F32),
            pltpu.SemaphoreType.DMA((4,)),
            pltpu.SemaphoreType.DMA((parts,)),
            pltpu.SemaphoreType.DMA((parts + 1,)),
        ],
        name="project",
    )(
        token_pair.reshape(tokens * band, depth),
        jnp.swapaxes(w_zpair, 0, 1),
        atom_single,
        atom_token,
        token_atoms,
        window_offset,
    )
    near = [(i, i ^ 1) for i in range(count)]
    far = [(i, ((i + 1) ^ 1) - 1) for i in range(1, count - 1)]
    first_side = lax.ppermute(payload, RING, near)
    second_side = lax.ppermute(payload, RING, far)

    in_hbm = pl.BlockSpec(memory_space=pltpu.HBM)
    small = (
        jnp.swapaxes(w_single, 1, 2),
        w_pair_mlp,
        jnp.swapaxes(w_bias, 1, 2),
    )
    large = (w_attn, w_out, w_trans_in, w_trans_out, w_token)
    reach = 3 * atoms
    windows = (atoms + 5 * HALO) // QB
    early, _, _ = window_split(windows)
    heads = w_bias.shape[2]
    channels_out = w_token.shape[1]

    def hbm(*arrays):
        return [pltpu.with_memory_space_constraint(x, pltpu.HBM) for x in arrays]

    pair_scratch = [
        pltpu.VMEM((3, payload_rows, width), BF16),
        *[pltpu.VMEM(w.shape, BF16) for w in small],
        pltpu.VMEM((8, LANES), jnp.int32),
        pltpu.SMEM((8, LANES), jnp.int32),
        pltpu.VMEM((3 * tiles + 1, 8, LANES), jnp.int32),
        pltpu.VMEM((3 * tiles + 1, channels, LANES), F32),
        pltpu.VMEM((reach, LANES), jnp.int32),
        pltpu.VMEM((reach, LANES), jnp.int32),
        pltpu.VMEM((3 * pairs * channels, LANES), F32),
        pltpu.VMEM((channels, reach, LANES), F32),
        pltpu.VMEM((PAIR_GROUP, channels, LANES), F32),
        pltpu.VMEM((PAIR_GROUP, QB, LANES), jnp.int32),
        pltpu.VMEM((PAIR_SLOTS, PAIR_GROUP, 256, 256), F32),
        *[pltpu.VMEM((PAIR_GROUP, 256, 256), BF16)] * 3,
        pltpu.VMEM((reach, 256), BF16),
        pltpu.VMEM((channels // 2, 256, 256), BF16),
        pltpu.VMEM((3, 256, 256), BF16),
        pltpu.VMEM((BLOCKS * heads * 256 // channels, 256), BF16),
        pltpu.VMEM((reach, width), F32),
        pltpu.VMEM((reach, LANES), F32),
        pltpu.SemaphoreType.DMA((7,)),
    ]
    early_bias = pl.pallas_call(
        early_kernel,
        out_shape=jax.ShapeDtypeStruct((early, BLOCKS, heads * QB, KW), F32),
        in_specs=[in_hbm, anywhere] + [in_hbm] * len(small),
        out_specs=vmem,
        scratch_shapes=pair_scratch,
        compiler_params=pltpu.CompilerParams(vmem_limit_bytes=40 * 2**20),
        cost_estimate=pl.CostEstimate(
            flops=2 * 10**9, transcendentals=10**5, bytes_accessed=8 * 10**6
        ),
        name="early_pairs",
    )(*hbm(payload), first_side, *hbm(*small))
    token_single, atom_out = pl.pallas_call(
        main_kernel,
        out_shape=(
            jax.ShapeDtypeStruct((tokens, channels_out), BF16),
            jax.ShapeDtypeStruct((atoms, width), BF16),
        ),
        in_specs=[in_hbm] + [anywhere] * 2 + [vmem] + [in_hbm] * (len(small) + len(large)),
        out_specs=(vmem, vmem),
        scratch_shapes=pair_scratch
        + [
            *[pltpu.VMEM(w.shape, BF16) for w in large],
            pltpu.VMEM((windows - early, BLOCKS, heads * QB, KW), F32),
            pltpu.VMEM((reach, width), BF16),
            pltpu.VMEM((reach, width), F32),
            pltpu.VMEM((reach, width), F32),
            pltpu.VMEM((reach, width), F32),
            pltpu.VMEM((reach, width), BF16),
            pltpu.VMEM((atoms + LANES, channels_out), BF16),
            pltpu.SemaphoreType.DMA((len(large),)),
        ],
        compiler_params=pltpu.CompilerParams(vmem_limit_bytes=48 * 2**20),
        name="encode",
    )(*hbm(payload), first_side, second_side, early_bias, *hbm(*small, *large))
    return token_single, atom_out


def solution(mesh):
    split = ("group", "seq", "chan", "sub")
    in_specs = (
        P(split, None),
        P(split),
        P(split),
        P(split),
        P(split, None, None),
        P(),
        P(),
        P(),
        P(),
        P(),
        P(),
        P(),
        P(),
        P(),
    )
    out_specs = (P(split, None), P(split, None))
    return jax.shard_map(shards, mesh=mesh, in_specs=in_specs, out_specs=out_specs, check_vma=False)
```
